512 devices in a mesh: band: 64 (over y, z), lev: 8 (over x, core).
Axes of the slice: x: 4, y: 8, z: 8, core: 2. Of those that a mesh axis runs over, the one named last changes fastest.
Arguments:
- concentration: float32 [4, 8, 128, 256], P(None, 'lev', 'band'), may hold values from 0.1 to 2
- target: float32 [4, 8, 128, 256], P(None, 'lev', 'band'), may hold values from -6 to 6
- zonal_wind: float32 [8, 128, 256], P('lev', 'band'), may hold values from -0.6 to 0.6
- merid_wind: float32 [8, 128, 256], P('lev', 'band'), may hold values from -0.6 to 0.6
- sea_mask: int32 [128, 256], P('band'), may hold values 0 or 1
- first_weight: float32 [2, 20, 128], replicated, may hold values from -1.25 to 1.25
- first_bias: float32 [2, 128], replicated, may hold values from -3 to 3
- middle_weight: float32 [2, 128, 128], replicated, may hold values from -0.5 to 0.5
- middle_bias: float32 [2, 128], replicated, may hold values from -3 to 3
- last_weight: float32 [2, 4, 128], replicated, may hold values from -0.125 to 0.125
- last_bias: float32 [2, 4], replicated, may hold values from -0.6 to 0.6
Outputs:
- final_field: float32 [4, 8, 128, 256], P(None, 'lev', 'band')
- first_weight_grad: float32 [2, 20, 128], replicated
- first_bias_grad: float32 [2, 128], replicated
- middle_weight_grad: float32 [2, 128, 128], replicated
- middle_bias_grad: float32 [2, 128], replicated
- last_weight_grad: float32 [2, 4, 128], replicated
- last_bias_grad: float32 [2, 4], replicated
The draws below stay inside these ranges and needn't reach their ends.
Inputs may be any that keep to these rules, and one draw needn't show every extreme that they name: `sea_mask`: 1 marks a sea cell, 0 a land cell.
All inputs are finite; a program needn't handle non-finite values. No bound on the sum of `sea_mask` on one device may be relied on, other than what follows from the above.
Results may differ from the reference program's by a relative error of at most 0.00013.
Values sent between devices are 32-bit elements; how exact they have to be, the bound alone decides.
A program may use at most 64 MiB of HBM per device.

```python
import math
import jax
import jax.numpy as jnp
from jax import lax

BINS = 4
WIDTH = 128
F_IN = 20
STEPS = 3
NX = 128
NY = 256
LEVELS = 8


def place_ends(drawn, key, smallest, largest):
    place = [jax.random.randint(jax.random.fold_in(key, axis), (), 0, length) for axis, length in enumerate(drawn.shape)]
    widest = drawn.shape.index(max(drawn.shape))
    next_to = place[:widest] + [(place[widest] + 1) % drawn.shape[widest]] + place[widest + 1:]
    return drawn.at[tuple(place)].set(smallest).at[tuple(next_to)].set(largest)


def levels(stream_key, dims, shards, low, high):
    gain = 1.0
    for axis_at, shards_of in shards:
        draws = jax.random.uniform(jax.random.fold_in(jax.random.fold_in(stream_key, 6), axis_at), (shards_of,), jnp.float32, low / len(shards), high / len(shards))
        gain = gain * jnp.repeat(jnp.exp(draws), dims[axis_at] // shards_of).reshape((-1,) + (1,) * (len(dims) - 1 - axis_at))
    return gain


def scatter_about(key, dims, spread, limit, shards=(), dtype=jnp.bfloat16):
    drawn = jax.random.normal(key, dims, jnp.float32) * spread
    if len(shards) > 0:
        drawn = levels(key, dims, shards, -0.22, 0.18) * drawn
    return jnp.clip(drawn, min=-limit, max=limit).astype(dtype)


def setup_inputs(seed: int = 0) -> dict:
    splits = jax.random.split(jax.random.key(seed), 12)
    concentration = jnp.clip(jnp.exp(math.log(2.0) - 2.9957323 * jax.random.uniform(splits[0], (BINS, LEVELS, NX, NY), jnp.float32) ** levels(splits[0], (BINS, LEVELS, NX, NY), ((1, 8), (2, 64)), -0.2, 0.2)), 0.1, 2.0)
    target = scatter_about(splits[1], (BINS, LEVELS, NX, NY), 1.0, 6.0, ((1, 8), (2, 64)), jnp.float32)
    zonal_wind = jnp.clip(jax.random.uniform(splits[2], (LEVELS, NX, NY), jnp.float32, -0.6, 0.6) * levels(splits[2], (LEVELS, NX, NY), ((0, 8), (1, 64)), -0.4, 0.0), -0.6, 0.6)
    merid_wind = jnp.clip(jax.random.uniform(splits[3], (LEVELS, NX, NY), jnp.float32, -0.6, 0.6) * levels(splits[3], (LEVELS, NX, NY), ((0, 8), (1, 64)), -0.4, 0.0), -0.6, 0.6)
    sea_mask = place_ends((jax.random.randint(splits[4], (NX, NY), 0, 4) < 3).astype(jnp.int32), jax.random.fold_in(splits[4], 1), 0, 1)
    first_weight = scatter_about(splits[5], (2, F_IN, WIDTH), F_IN ** -0.5, 1.25, (), jnp.float32)
    first_bias = scatter_about(splits[6], (2, WIDTH), 0.5, 3.0, (), jnp.float32)
    middle_weight = scatter_about(splits[7], (2, WIDTH, WIDTH), WIDTH ** -0.5, 0.5, (), jnp.float32)
    middle_bias = scatter_about(splits[8], (2, WIDTH), 0.5, 3.0, (), jnp.float32)
    last_weight = scatter_about(splits[9], (2, 4, WIDTH), (16 * WIDTH) ** -0.5, 0.125, (), jnp.float32)
    last_bias = scatter_about(splits[10], (2, 4), 0.1, 0.6, (), jnp.float32)
    return {"concentration": concentration, "target": target, "zonal_wind": zonal_wind, "merid_wind": merid_wind, "sea_mask": sea_mask, "first_weight": first_weight, "first_bias": first_bias, "middle_weight": middle_weight, "middle_bias": middle_bias, "last_weight": last_weight, "last_bias": last_bias}


stencil_base = (-1.0 / 12.0, 7.0 / 12.0, 7.0 / 12.0, -1.0 / 12.0)

def cut_along(array, direction, start, length):
    return lax.slice_in_dim(array, start, start + length, axis=direction)

def pad_along(array, direction, width):
    widths = [(0, 0)] * array.ndim
    widths[direction] = (width, width)
    return jnp.pad(array, widths)

def face_flux(network, stencil, courant, mask_low, mask_high):
    w_first, b_first, w_second, b_second, w_last, b_last = network
    face_shape = courant.shape
    columns = courant.size
    nbins = stencil.shape[1]
    features = jnp.concatenate([stencil.reshape(4 * nbins, columns), courant.reshape(1, columns), (courant * courant).reshape(1, columns), jnp.broadcast_to(mask_low, face_shape).reshape(1, columns), jnp.broadcast_to(mask_high, face_shape).reshape(1, columns)], 0)
    hidden_one = jnp.tanh(jnp.dot(w_first.T, features, precision=lax.Precision.HIGHEST) + b_first[:, None])
    hidden_two = jnp.tanh(jnp.dot(w_second.T, hidden_one, precision=lax.Precision.HIGHEST) + b_second[:, None])
    output = jnp.dot(w_last, hidden_two, precision=lax.Precision.HIGHEST) + b_last[:, None]
    correction = output - lax.optimization_barrier(jnp.mean(output, 0, keepdims=True))
    weights_face = jnp.asarray(stencil_base, jnp.float32)[:, None] + correction
    face_value = lax.optimization_barrier(jnp.sum(weights_face.reshape((4, 1) + face_shape) * stencil, 0))
    return courant[None] * face_value

def advance(network, padded, wind_padded, mask_padded, direction):
    length = padded.shape[direction] - 4
    stencil = jnp.stack([cut_along(padded, direction, offset, length + 1) for offset in range(4)])
    courant = 0.5 * (cut_along(wind_padded, direction - 1, 0, length + 1) + cut_along(wind_padded, direction - 1, 1, length + 1))
    mask_low = cut_along(mask_padded, direction - 1, 0, length + 1)
    mask_high = cut_along(mask_padded, direction - 1, 1, length + 1)
    fluxes = face_flux(network, stencil, courant, mask_low, mask_high)
    centre = cut_along(padded, direction, 2, length)
    return centre - (cut_along(fluxes, direction, 1, length) - cut_along(fluxes, direction, 0, length))

def sweep_all(network, field, wind, sea_field, direction):
    mask_padded = pad_along(sea_field, direction - 1, 1)

    def level_sweep(pair):
        level_field, level_wind = pair
        padded = pad_along(level_field[:, None], direction, 2)
        wind_padded = pad_along(level_wind[None], direction - 1, 1)
        return advance(network, padded, wind_padded, mask_padded, direction)[:, 0]
    result = lax.map(jax.checkpoint(level_sweep), (jnp.moveaxis(field, 1, 0), wind))
    return jnp.moveaxis(result, 0, 1)

def reference(concentration, target, zonal_wind, merid_wind, sea_mask, first_weight, first_bias, middle_weight, middle_bias, last_weight, last_bias):
    sea_field = sea_mask.astype(jnp.float32)[None]
    params = (first_weight, first_bias, middle_weight, middle_bias, last_weight, last_bias)
    loss_scale = 1.0 / math.sqrt(BINS * LEVELS * NX * NY)

    def forward(weights):
        zonal_net = tuple((member[0] for member in weights))
        merid_net = tuple((member[1] for member in weights))
        field = concentration
        for step_number in range(STEPS):
            field = sweep_all(zonal_net, field, zonal_wind, sea_field, 3)
            field = sweep_all(merid_net, field, merid_wind, sea_field, 2)
        error = field - target
        return (0.5 * loss_scale * jnp.sum(error * error), field)
    grads, final = jax.grad(forward, has_aux=True)(params)
    return (final, grads[0], grads[1], grads[2], grads[3], grads[4], grads[5])
```

```python
import functools
import math

import jax
import jax.numpy as jnp
from jax import lax
from jax.experimental import pallas as pl
from jax.experimental.pallas import tpu as pltpu
from jax.sharding import PartitionSpec as P

STEPS = 3
WIDTH = 128
F32 = jnp.float32
BF16 = jnp.bfloat16
MESH = pl.DeviceIdType.MESH
BASE = (-1.0 / 12.0, 7.0 / 12.0, 7.0 / 12.0, -1.0 / 12.0)

NY = 256
GAP = 64
NZ = 640
SLOT_FACE = (1, 2, 3, 0, 4)
NM = 5 * NY
NET_ROWS = 160
GRAD_ROWS = 2 * NET_ROWS


def split(x):
    hi = x.astype(BF16)
    lo = (x - hi.astype(F32)).astype(BF16)
    return hi, lo


def stack(x):
    return jnp.concatenate(split(x), axis=0)


def dot(a, b):
    return lax.dot_general(a, b, (((1,), (0,)), ((), ())), preferred_element_type=F32)


def dot_nt(a, b):
    return lax.dot_general(a, b, (((1,), (1,)), ((), ())), preferred_element_type=F32)


def low_half(shape):
    return lax.broadcasted_iota(jnp.int32, shape, 0) < 4


def pick(a, b):
    return jnp.where(low_half(a.shape), a, b)


def turn(x):
    return pltpu.roll(x, 4, axis=0)


def lane_roll(x, shift):
    return pltpu.roll(x, shift % x.shape[1], axis=1)


def both_rows(block):
    turned = turn(block)
    return pick(block, turned), pick(turned, block)


def to_line(first, second):
    gap = jnp.zeros((first.shape[0], 2 * GAP), F32)
    return jnp.concatenate([lane_roll(jnp.concatenate([first, gap], 1), GAP), second], 1)


def from_line(line):
    return lane_roll(line[:, : NY + 2 * GAP], -GAP)[:, :NY], line[:, NY + 2 * GAP :]


def kernel(
    bands,
    levs,
    loss_scale,
    conc_ref,
    target_ref,
    zwind_ref,
    mwind_ref,
    sea_ref,
    w1_ref,
    b1_ref,
    w2_ref,
    b2_ref,
    w3_ref,
    b3_ref,
    field_ref,
    gw1_ref,
    gb1_ref,
    gw2_ref,
    gb2_ref,
    gw3_ref,
    gb3_ref,
    w1s,
    w2s,
    w3s,
    w3e,
    w2b,
    w1b,
    b2s,
    b3s,
    zcour,
    mcour,
    halo,
    ghalo,
    winds,
    line,
    gline,
    ax_z,
    ax_m,
    h2_z,
    h2_m,
    s1_z,
    s1_m,
    s2_z,
    s2_m,
    st_z,
    st_m,
    cf_z,
    cf_m,
    d1_z,
    d1_m,
    d2_z,
    d2_m,
    pb_z,
    pb_m,
    acc2,
    acc1,
    acc3,
    accb2,
    accp,
    grads,
    r1,
    s1buf,
    r2,
    r3,
    a4,
    full,
    halo_send,
    halo_recv,
    ghalo_send,
    ghalo_recv,
    wind_send,
    wind_recv,
    red_send,
    red_recv,
):
    side_y = math.isqrt(bands)
    side_z = bands // side_y
    band = lax.axis_index("band")
    lev = lax.axis_index("lev")
    my_y = band // side_z
    my_z = band % side_z

    def y_device(ty):
        return {"band": ty * side_z + my_z, "lev": lev}

    def z_device(tz):
        return {"band": my_y * side_z + tz, "lev": lev}

    def lev_device(tl):
        return {"band": band, "lev": tl}

    def band_device(tb):
        return {"band": tb, "lev": lev}

    winds[...] = jnp.zeros_like(winds)
    halo[...] = jnp.zeros_like(halo)
    ghalo[...] = jnp.zeros_like(ghalo)
    barrier = pltpu.get_barrier_semaphore()
    greeted = 0
    for delta in (1, bands - 1, 2, bands - 2):
        pl.semaphore_signal(
            barrier, inc=1, device_id=band_device((band + delta) % bands), device_id_type=MESH
        )
        greeted += 1
    for d in range(1, levs):
        pl.semaphore_signal(
            barrier, inc=1, device_id=lev_device((lev + d) % levs), device_id_type=MESH
        )
        greeted += 1
    for d in range(1, side_y):
        pl.semaphore_signal(
            barrier, inc=1, device_id=y_device((my_y + d) % side_y), device_id_type=MESH
        )
        greeted += 1
    for d in range(1, side_z):
        pl.semaphore_signal(
            barrier, inc=1, device_id=z_device((my_z + d) % side_z), device_id_type=MESH
        )
        greeted += 1

    def prepare(net):
        w1 = w1_ref[net]
        b1 = b1_ref[net : net + 1, :]
        rows = jnp.concatenate([w1, b1, jnp.zeros((11, WIDTH), F32)], 0)
        hi, lo = split(rows)
        hi, lo = hi.astype(F32), lo.astype(F32)
        w1s[net] = jnp.concatenate([hi, hi, lo, jnp.zeros_like(hi)], 0).T.astype(BF16)
        hi, lo = split(rows[0:16])
        w1b[net, 0:16, 0:128] = hi
        w1b[net, 0:16, 128:256] = hi
        w1b[net, 16:32, 0:128] = lo
        w1b[net, 16:32, 128:256] = lo
        w2 = w2_ref[net]
        for ref, mat in ((w2s, w2.T), (w2b, w2)):
            hi, lo = split(mat)
            ref[net, 0:128, 0:128] = hi
            ref[net, 0:128, 128:256] = hi
            ref[net, 128:256, 0:128] = lo
            ref[net, 128:256, 128:256] = lo
        b2s[net] = jnp.broadcast_to(b2_ref[net : net + 1, :], (WIDTH, WIDTH)).T
        w3 = w3_ref[net]
        w3 = w3 - jnp.mean(w3, 0, keepdims=True)
        group = lax.broadcasted_iota(jnp.int32, (16, WIDTH), 0) // 4
        rep = jnp.zeros((16, WIDTH), F32)
        for j in range(4):
            rep = jnp.where(group == j, w3[j : j + 1, :], rep)
        hi, lo = split(rep)
        w3s[net, 0:16, 0:128] = hi
        w3s[net, 0:16, 128:256] = hi
        w3s[net, 16:32, 0:128] = lo
        w3s[net, 16:32, 128:256] = lo
        hi, lo = hi.astype(F32), lo.astype(F32)
        w3e[net] = jnp.concatenate([hi, hi, lo, jnp.zeros((80, WIDTH), F32)], 0).T.astype(BF16)
        b3 = b3_ref[net : net + 1, :]
        b3 = b3 - jnp.mean(b3, 1, keepdims=True)
        mine = (
            lax.broadcasted_iota(jnp.int32, (16, 4), 0) // 4
            == lax.broadcasted_iota(jnp.int32, (16, 4), 1)
        )
        column = jnp.sum(jnp.where(mine, b3, 0.0), 1, keepdims=True)
        place = lax.broadcasted_iota(jnp.int32, (16, WIDTH), 0) // 4
        base = jnp.where((place == 0) | (place == 3), BASE[0], BASE[1])
        b3s[net] = column + base

    def constant_rows(ref, lo_lane, courant, low, high):
        n = courant.shape[1]
        place = lax.broadcasted_iota(jnp.int32, (16, n), 0)
        rows = jnp.where(place == 0, courant, 0.0)
        rows = jnp.where(place == 1, courant * courant, rows)
        rows = jnp.where(place == 2, low, rows)
        rows = jnp.where(place == 3, high, rows)
        rows = jnp.where(place == 4, 1.0, rows)
        hi, lo = split(rows)
        for s in range(STEPS):
            ref[s, 272:288, lo_lane : lo_lane + n] = hi
            ref[s, 304:320, lo_lane : lo_lane + n] = lo
            ref[s, 336:352, lo_lane : lo_lane + n] = hi

    def forward(net, s, lanes, stencil, courant, ax, h2, s1, s2, st, cf):
        hi, lo = split(stencil)
        ax[s, 256:272, lanes] = hi
        ax[s, 288:304, lanes] = lo
        ax[s, 320:336, lanes] = hi
        st[s, :, lanes] = stencil
        one = jnp.tanh(dot(w1s[net, :, 0:96], ax[s, 256:352, lanes]))
        s1[s, :, lanes] = 1.0 - one * one
        pair = stack(one)
        ax[s, 0:256, lanes] = pair
        out = dot(w2s[net], pair)
        bias = b2s[net]
        n = out.shape[1]
        bias = jnp.concatenate([bias] * (n // WIDTH), 1)
        two = jnp.tanh(out[0:128] + out[128:256] + bias)
        s2[s, :, lanes] = 1.0 - two * two
        pair = stack(two)
        h2[s, :, lanes] = pair
        out = dot(w3s[net], pair)
        coef = out[0:16] + out[16:32] + jnp.concatenate([b3s[net]] * (n // WIDTH), 1)
        cf[s, :, lanes] = coef
        terms = coef * stencil
        half = terms[0:8] + terms[8:16]
        return courant * (half + turn(half))

    def backward(net, s, lanes, dflux, courant, d1, d2, pb, s1, s2, st, cf):
        dq = courant * dflux
        dq = jnp.concatenate([dq, dq], 0)
        weighted = dq * st[s, :, lanes]
        hi, lo = split(weighted)
        pb[0:16, lanes] = hi
        pb[16:32, lanes] = lo
        two = dot(w3e[net, :, 0:48], jnp.concatenate([hi, lo, hi], 0)) * s2[s, :, lanes]
        pair = stack(two)
        d2[:, lanes] = pair
        out = dot(w2b[net], pair)
        one = (out[0:128] + out[128:256]) * s1[s, :, lanes]
        pair = stack(one)
        d1[:, lanes] = pair
        out = dot(w1b[net], pair)
        return out[0:16] + out[16:32] + cf[s, :, lanes] * dq, weighted

    def quads(x, m, n):
        return (x[0:m, 0:n] + x[m : 2 * m, n : 2 * n]) + (x[0:m, n : 2 * n] + x[m : 2 * m, 0:n])

    def weight_grads(net, s, lanes, ax, h2, d1, d2, pb):
        out = dot_nt(ax[s, 0:288, lanes], d2[:, lanes])
        acc2[net] += quads(out, 128, 128)
        accb2[net] += out[256:288, 0:128] + out[256:288, 128:256]
        out = dot_nt(ax[s, 256:320, lanes], d1[:, lanes])
        acc1[net] += quads(out, 32, 128)
        out = dot_nt(pb[:, lanes], h2[s, :, lanes])
        acc3[net] += quads(out, 16, 128)

    def lane_fold(x):
        out = x[:, 0:128]
        for i in range(1, x.shape[1] // 128):
            out = out + x[:, 128 * i : 128 * (i + 1)]
        return out

    zchunks = (slice(0, 256), slice(256, 512), slice(512, 640))

    def zonal_stencil():
        c = line[...]
        return jnp.concatenate(
            [pick(lane_roll(c, 1), c), pick(lane_roll(c, -1), lane_roll(c, -2))], 0
        )

    def zonal(s):
        stencil = zonal_stencil()
        parts = [
            forward(
                0, s, lanes, stencil[:, lanes], zcour[:, lanes], ax_z, h2_z, s1_z, s2_z, st_z, cf_z
            )
            for lanes in zchunks
        ]
        flux = jnp.concatenate(parts, 1)
        new = line[...] - (flux - lane_roll(flux, 1))
        halo[s, 2] = pick(*from_line(new))

    def face_stencil(s, face):
        mid = turn(halo[s, 2])
        if face == 1:
            return jnp.concatenate([halo[s, 1], halo[s, 2]], 0)
        if face == 3:
            return jnp.concatenate([halo[s, 2], halo[s, 3]], 0)
        if face == 2:
            return jnp.concatenate([pick(turn(halo[s, 1]), mid), pick(mid, turn(halo[s, 3]))], 0)
        if face == 0:
            before = turn(halo[s, 1])
            return jnp.concatenate([pick(turn(halo[s, 0]), before), pick(before, mid)], 0)
        after = turn(halo[s, 3])
        return jnp.concatenate([pick(mid, after), pick(after, turn(halo[s, 4]))], 0)

    def merid_faces(s, slots):
        fluxes = []
        for slot in slots:
            lanes = slice(slot * NY, (slot + 1) * NY)
            fluxes.append(
                forward(
                    1,
                    s,
                    lanes,
                    face_stencil(s, SLOT_FACE[slot]),
                    mcour[:, lanes],
                    ax_m,
                    h2_m,
                    s1_m,
                    s2_m,
                    st_m,
                    cf_m,
                )
            )
        return fluxes

    def halo_copy(buf, s, which, send, recv):
        delta, slot = ((1, 1), (-1, 3), (2, 0), (-2, 4))[which]
        return pltpu.make_async_remote_copy(
            src_ref=buf.at[s, 2],
            dst_ref=buf.at[s, slot],
            send_sem=send.at[s, which],
            recv_sem=recv.at[s, which],
            device_id=band_device(band + delta),
            device_id_type=MESH,
        )

    has_target = (band < bands - 1, band >= 1, band < bands - 2, band >= 2)
    has_source = (band >= 1, band < bands - 1, band >= 2, band < bands - 2)

    def halo_start(buf, s, send, recv, which_all):
        for which in which_all:

            @pl.when(has_target[which])
            def _():
                halo_copy(buf, s, which, send, recv).start()

    def halo_wait(buf, s, send, recv, which_all):
        for which in which_all:

            @pl.when(has_source[which])
            def _():
                halo_copy(buf, s, which, send, recv).wait_recv()

    def halo_drain(buf, s, send, recv, which_all):
        for which in which_all:

            @pl.when(has_target[which])
            def _():
                halo_copy(buf, s, which, send, recv).wait_send()

    prepare(0)
    rows = [conc_ref[b, 0, r : r + 1, :] for r in range(2) for b in range(4)]
    line[...] = to_line(*both_rows(jnp.concatenate(rows, 0)))
    sea = sea_ref[...].astype(F32)
    zw = to_line(zwind_ref[0, 0:1, :], zwind_ref[0, 1:2, :])
    zs = to_line(sea[0:1, :], sea[1:2, :])
    courant = 0.5 * (zw + lane_roll(zw, -1))
    zcour[...] = jnp.broadcast_to(courant, (8, NZ))
    constant_rows(ax_z, 0, courant, zs, lane_roll(zs, -1))
    winds[0, 2, 0:2, :] = mwind_ref[0]
    winds[0, 2, 2:4, :] = sea
    for acc in (acc2, acc1, acc3, accb2, accp):
        acc[...] = jnp.zeros_like(acc)

    def forward_step(s, carry):
        zonal(s)

        @pl.when(s == 0)
        def _():
            pl.semaphore_wait(barrier, greeted)
            halo_start(winds, 0, wind_send, wind_recv, (0, 1))

        halo_start(halo, s, halo_send, halo_recv, (0, 1, 2, 3))

        @pl.when(s == 0)
        def _():
            prepare(1)
            halo_wait(winds, 0, wind_send, wind_recv, (0, 1))
            w = [winds[0, 1 + i // 2, i % 2 : i % 2 + 1, :] for i in range(6)]
            m = [winds[0, 1 + i // 2, 2 + i % 2 : 3 + i % 2, :] for i in range(6)]
            for slot, face in enumerate(SLOT_FACE):
                courant = 0.5 * (w[face] + w[face + 1])
                mcour[:, slot * NY : (slot + 1) * NY] = jnp.broadcast_to(courant, (8, NY))
                constant_rows(ax_m, slot * NY, courant, m[face], m[face + 1])

        @pl.when(s > 0)
        def _():
            halo_wait(halo, s - 1, halo_send, halo_recv, (2, 3))
            merid_faces(s - 1, (3, 4))

        halo_wait(halo, s, halo_send, halo_recv, (0, 1))
        f1, f2, f3 = merid_faces(s, (0, 1, 2))
        new = halo[s, 2] - pick(f2 - f1, f3 - f2)
        line[...] = to_line(*both_rows(new))

        @pl.when(s == STEPS - 1)
        def _():
            rows = [target_ref[b, 0, r : r + 1, :] for r in range(2) for b in range(4)]
            ghalo[STEPS - 1, 2] = (new - jnp.concatenate(rows, 0)) * loss_scale
            halo_start(ghalo, STEPS - 1, ghalo_send, ghalo_recv, (0, 1))
            for r in range(2):
                for b in range(4):
                    field_ref[b, 0, r : r + 1, :] = new[4 * r + b : 4 * r + b + 1, :]

        return carry

    lax.fori_loop(0, STEPS, forward_step, 0)
    halo_wait(halo, STEPS - 1, halo_send, halo_recv, (2, 3))
    merid_faces(STEPS - 1, (3, 4))

    def backward_step(i, carry):
        s = STEPS - 1 - i
        halo_wait(ghalo, s, ghalo_send, ghalo_recv, (0, 1))
        g = []
        for block in (1, 2, 3):
            g.extend(both_rows(ghalo[s, block]))
        lows, highs = [None] * 5, [None] * 5
        first = None
        inner = None
        for slot, face in enumerate(SLOT_FACE):
            lanes = slice(slot * NY, (slot + 1) * NY)
            out, weighted = backward(
                1,
                s,
                lanes,
                g[face + 1] - g[face],
                mcour[:, lanes],
                d1_m,
                d2_m,
                pb_m,
                s1_m,
                s2_m,
                st_m,
                cf_m,
            )
            lows[face], highs[face] = out[0:8], out[8:16]
            if slot == 0:
                first = lane_fold(weighted)
            elif slot == 1:
                inner = lane_fold(weighted)
            elif slot == 2:
                inner = inner + lane_fold(weighted)
        new = ghalo[s, 2] + (highs[1] + lows[3])
        new = new + turn(pick(highs[2] + lows[4], highs[0] + lows[2]))
        accp[1] += inner

        @pl.when(band == 0)
        def _():
            accp[1] += first

        gline[...] = to_line(*both_rows(new))
        gz = gline[...]
        dflux = lane_roll(gz, -1) - gz
        outs = [
            backward(
                0,
                s,
                lanes,
                dflux[:, lanes],
                zcour[:, lanes],
                d1_z,
                d2_z,
                pb_z,
                s1_z,
                s2_z,
                st_z,
                cf_z,
            )
            for lanes in zchunks
        ]
        out = jnp.concatenate([o[0] for o in outs], 1)
        low, high = out[0:8], out[8:16]
        t = pick(lane_roll(low, -1), low) + pick(lane_roll(high, 1), lane_roll(high, 2))
        new = gz + t + turn(t)

        @pl.when(s > 0)
        def _():
            ghalo[jnp.maximum(s - 1, 0), 2] = pick(*from_line(new))
            halo_start(ghalo, s - 1, ghalo_send, ghalo_recv, (0, 1))

        accp[0] += sum(lane_fold(o[1]) for o in outs)
        weight_grads(1, s, slice(NY, 3 * NY), ax_m, h2_m, d1_m, d2_m, pb_m)

        @pl.when(band == 0)
        def _():
            weight_grads(1, s, slice(0, NY), ax_m, h2_m, d1_m, d2_m, pb_m)

        weight_grads(0, s, slice(0, NZ), ax_z, h2_z, d1_z, d2_z, pb_z)
        return carry

    lax.fori_loop(0, STEPS, backward_step, 0)

    centre = jnp.where(
        lax.broadcasted_iota(jnp.int32, (16, 16), 1) // 4
        == lax.broadcasted_iota(jnp.int32, (16, 16), 0),
        0.75,
        -0.25,
    )
    centre = jnp.concatenate([centre, centre], 1).astype(BF16)
    for net in range(2):
        top = net * NET_ROWS
        grads[top : top + 128] = acc2[net]
        grads[top + 128 : top + 160] = acc1[net]
        grads[top + 149 : top + 150] = accb2[net, 20:21, :]
        grads[top + 152 : top + 156] = dot(centre, stack(acc3[net]))[0:4]
        sums = jnp.sum(accp[net], 1, keepdims=True)
        mine = (
            lax.broadcasted_iota(jnp.int32, (16, WIDTH), 0) // 4
            == lax.broadcasted_iota(jnp.int32, (16, WIDTH), 1)
        )
        row = jnp.sum(jnp.where(mine, sums, 0.0), 0, keepdims=True)
        grads[top + 156 : top + 157] = row - jnp.sum(row, 1, keepdims=True) * 0.25

    piece = GRAD_ROWS // levs
    part = piece // side_y
    started = []

    def send(src, dst, index, device):
        copy = pltpu.make_async_remote_copy(
            src_ref=src,
            dst_ref=dst,
            send_sem=red_send.at[index],
            recv_sem=red_recv.at[index],
            device_id=device,
            device_id_type=MESH,
        )
        copy.start()
        started.append(copy)
        return copy

    def wait(copies):
        for copy in copies:
            copy.wait_recv()

    at = 0
    copies = []
    for d in range(1, levs):
        tl = (lev + d) % levs
        src = grads.at[pl.ds(pl.multiple_of(tl * piece, 8), piece)]
        copies.append(send(src, r1.at[d - 1], at, lev_device(tl)))
        at += 1
    total = grads[pl.ds(pl.multiple_of(lev * piece, 8), piece)]
    wait(copies)
    for d in range(1, levs):
        total = total + r1[d - 1]
    for i in range(side_y):
        s1buf[i] = total[i * part : (i + 1) * part]
    copies = []
    for d in range(1, side_y):
        ty = (my_y + d) % side_y
        copies.append(send(s1buf.at[ty], r2.at[d - 1], at, y_device(ty)))
        at += 1
    total = s1buf[my_y]
    wait(copies)
    for d in range(1, side_y):
        total = total + r2[d - 1]
    r3[my_z] = total
    copies = []
    for d in range(1, side_z):
        tz = (my_z + d) % side_z
        copies.append(send(r3.at[my_z], r3.at[my_z], at, z_device(tz)))
        at += 1
    wait(copies)
    total = r3[0]
    for i in range(1, side_z):
        total = total + r3[i]
    a4[my_y] = total
    copies = []
    for d in range(1, side_y):
        ty = (my_y + d) % side_y
        copies.append(send(a4.at[my_y], a4.at[my_y], at, y_device(ty)))
        at += 1
    wait(copies)
    for i in range(side_y):
        full[lev, i * part : (i + 1) * part] = a4[i]
    copies = []
    for d in range(1, levs):
        tl = (lev + d) % levs
        copies.append(send(full.at[lev], full.at[lev], at, lev_device(tl)))
        at += 1
    wait(copies)
    everything = full[...].reshape(GRAD_ROWS, WIDTH)
    for net in range(2):
        top = net * NET_ROWS
        gw2_ref[net] = everything[top : top + 128]
        gw1_ref[net] = everything[top + 128 : top + 148]
        gb1_ref[net : net + 1] = everything[top + 148 : top + 149]
        gb2_ref[net : net + 1] = everything[top + 149 : top + 150]
        gw3_ref[net] = everything[top + 152 : top + 156]
        gb3_ref[net : net + 1] = everything[top + 156 : top + 157, 0:4]

    for copy in started:
        copy.wait_send()
    halo_drain(winds, 0, wind_send, wind_recv, (0, 1))
    for s in range(STEPS):
        halo_drain(halo, s, halo_send, halo_recv, (0, 1, 2, 3))
        halo_drain(ghalo, s, ghalo_send, ghalo_recv, (0, 1))


def on_device(bands, levs, loss_scale, *args):
    piece = GRAD_ROWS // levs
    side_y = math.isqrt(bands)
    side_z = bands // side_y
    part = piece // side_y
    reductions = 2 * (levs - 1) + 2 * (side_y - 1) + (side_z - 1)
    vmem = pltpu.VMEM
    sweeps = [NZ, NM]
    scratch = [
        vmem((2, 128, 128), BF16),
        vmem((2, 256, 256), BF16),
        vmem((2, 32, 256), BF16),
        vmem((2, 128, 128), BF16),
        vmem((2, 256, 256), BF16),
        vmem((2, 32, 256), BF16),
        vmem((2, 128, 128), F32),
        vmem((2, 16, 128), F32),
        vmem((8, NZ), F32),
        vmem((8, NM), F32),
        vmem((STEPS, 5, 8, NY), F32),
        vmem((STEPS, 5, 8, NY), F32),
        vmem((1, 5, 8, NY), F32),
        vmem((8, NZ), F32),
        vmem((8, NZ), F32),
        *[vmem((STEPS, 352, n), BF16) for n in sweeps],
        *[vmem((STEPS, 256, n), BF16) for n in sweeps],
        *[vmem((STEPS, 128, n), F32) for n in sweeps],
        *[vmem((STEPS, 128, n), F32) for n in sweeps],
        *[vmem((STEPS, 16, n), F32) for n in sweeps],
        *[vmem((STEPS, 16, n), F32) for n in sweeps],
        *[vmem((256, n), BF16) for n in sweeps],
        *[vmem((256, n), BF16) for n in sweeps],
        *[vmem((32, n), BF16) for n in sweeps],
        vmem((2, 128, 128), F32),
        vmem((2, 32, 128), F32),
        vmem((2, 16, 128), F32),
        vmem((2, 32, 128), F32),
        vmem((2, 16, 128), F32),
        vmem((GRAD_ROWS, 128), F32),
        vmem((levs - 1, piece, 128), F32),
        vmem((side_y, part, 128), F32),
        vmem((side_y - 1, part, 128), F32),
        vmem((side_z, part, 128), F32),
        vmem((side_y, part, 128), F32),
        vmem((levs, piece, 128), F32),
        pltpu.SemaphoreType.DMA((STEPS, 4)),
        pltpu.SemaphoreType.DMA((STEPS, 4)),
        pltpu.SemaphoreType.DMA((STEPS, 4)),
        pltpu.SemaphoreType.DMA((STEPS, 4)),
        pltpu.SemaphoreType.DMA((1, 4)),
        pltpu.SemaphoreType.DMA((1, 4)),
        pltpu.SemaphoreType.DMA((reductions,)),
        pltpu.SemaphoreType.DMA((reductions,)),
    ]
    out_shape = [jax.ShapeDtypeStruct(args[0].shape, F32)] + [
        jax.ShapeDtypeStruct(args[i].shape, F32) for i in range(5, 11)
    ]
    return tuple(
        pl.pallas_call(
            functools.partial(kernel, bands, levs, loss_scale),
            out_shape=out_shape,
            in_specs=[pl.BlockSpec(memory_space=pltpu.VMEM)] * 11,
            out_specs=[pl.BlockSpec(memory_space=pltpu.VMEM)] * 7,
            scratch_shapes=scratch,
            compiler_params=pltpu.CompilerParams(
                collective_id=0, has_side_effects=True, vmem_limit_bytes=48 * 1024 * 1024
            ),
            name="advection_step",
        )(*args)
    )


def solution(mesh):
    bands, levs = mesh.shape["band"], mesh.shape["lev"]
    loss_scale = 1.0 / math.sqrt(4 * levs * 2 * bands * NY)
    return jax.shard_map(
        functools.partial(on_device, bands, levs, loss_scale),
        mesh=mesh,
        in_specs=(
            P(None, "lev", "band", None),
            P(None, "lev", "band", None),
            P("lev", "band", None),
            P("lev", "band", None),
            P("band", None),
            P(),
            P(),
            P(),
            P(),
            P(),
            P(),
        ),
        out_specs=(P(None, "lev", "band", None), P(), P(), P(), P(), P(), P()),
        check_vma=False,
    )
```

```python
import functools
import math

import jax
import jax.numpy as jnp
from jax import lax
from jax.experimental import pallas as pl
from jax.experimental.pallas import tpu as pltpu
from jax.sharding import PartitionSpec as P

STEPS = 3
WIDTH = 128
F32 = jnp.float32
BF16 = jnp.bfloat16
MESH = pl.DeviceIdType.MESH
BASE = (-1.0 / 12.0, 7.0 / 12.0, 7.0 / 12.0, -1.0 / 12.0)

NY = 256
GAP = 64
NZ = 640
SLOT_FACE = (1, 2, 3, 0, 4)
NM = 5 * NY
NET_ROWS = 160
GRAD_ROWS = 2 * NET_ROWS


def split(x):
    hi = x.astype(BF16)
    lo = (x - hi.astype(F32)).astype(BF16)
    return hi, lo


def stack(x):
    return jnp.concatenate(split(x), axis=0)


def dot(a, b):
    return lax.dot_general(a, b, (((1,), (0,)), ((), ())), preferred_element_type=F32)


def dot_nt(a, b):
    return lax.dot_general(a, b, (((1,), (1,)), ((), ())), preferred_element_type=F32)


def run(parts, skew=0):
    results = [None] * len(parts)
    live = set(range(len(parts)))
    tick = 0
    while live:
        for i in sorted(live):
            if tick >= i * skew:
                try:
                    next(parts[i])
                except StopIteration as stop:
                    results[i] = stop.value
                    live.discard(i)
        tick += 1
    return results


def low_half(shape):
    return lax.broadcasted_iota(jnp.int32, shape, 0) < 4


def pick(a, b):
    return jnp.where(low_half(a.shape), a, b)


def turn(x):
    return pltpu.roll(x, 4, axis=0)


def lane_roll(x, shift):
    return pltpu.roll(x, shift % x.shape[1], axis=1)


def both_rows(block):
    turned = turn(block)
    return pick(block, turned), pick(turned, block)


def to_line(first, second):
    gap = jnp.zeros((first.shape[0], 2 * GAP), F32)
    return jnp.concatenate([lane_roll(jnp.concatenate([first, gap], 1), GAP), second], 1)


def from_line(line):
    return lane_roll(line[:, : NY + 2 * GAP], -GAP)[:, :NY], line[:, NY + 2 * GAP :]


def kernel(
    bands,
    levs,
    loss_scale,
    conc_hbm,
    target_hbm,
    zwind_hbm,
    mwind_hbm,
    sea_hbm,
    w1_hbm,
    b1_hbm,
    w2_hbm,
    b2_hbm,
    w3_hbm,
    b3_hbm,
    field_ref,
    gw1_ref,
    gb1_ref,
    gw2_ref,
    gb2_ref,
    gw3_ref,
    gb3_ref,
    conc_ref,
    target_ref,
    zwind_ref,
    mwind_ref,
    sea_ref,
    w1_ref,
    b1_ref,
    w2_ref,
    b2_ref,
    w3_ref,
    b3_ref,
    input_sem,
    w1s,
    w2s,
    w3s,
    w3e,
    w2b,
    w1b,
    b2s,
    b3s,
    zcour,
    mcour,
    halo,
    ghalo,
    winds,
    line,
    gline,
    ax_z,
    ax_m,
    h2_z,
    h2_m,
    s1_z,
    s1_m,
    s2_z,
    s2_m,
    st_z,
    st_m,
    cf_z,
    cf_m,
    d1_z,
    d1_m,
    d2_z,
    d2_m,
    pb_z,
    pb_m,
    acc2,
    acc1,
    acc3,
    accb2,
    accp,
    grads,
    r1,
    s1buf,
    r2,
    r3,
    a4,
    full,
    halo_send,
    halo_recv,
    ghalo_send,
    ghalo_recv,
    wind_send,
    wind_recv,
    red_send,
    red_recv,
    first_send,
    first_recv,
):
    side_y = math.isqrt(bands)
    side_z = bands // side_y
    band = lax.axis_index("band")
    lev = lax.axis_index("lev")
    my_y = band // side_z
    my_z = band % side_z

    def y_device(ty):
        return {"band": ty * side_z + my_z, "lev": lev}

    def z_device(tz):
        return {"band": my_y * side_z + tz, "lev": lev}

    def lev_device(tl):
        return {"band": band, "lev": tl}

    def band_device(tb):
        return {"band": tb, "lev": lev}

    inputs = [
        pltpu.make_async_copy(src, dst, input_sem.at[i])
        for i, (src, dst) in enumerate(
            (
                (w2_hbm, w2_ref),
                (w1_hbm, w1_ref),
                (b1_hbm, b1_ref),
                (b2_hbm, b2_ref),
                (w3_hbm, w3_ref),
                (b3_hbm, b3_ref),
                (conc_hbm, conc_ref),
                (zwind_hbm, zwind_ref),
                (sea_hbm, sea_ref),
                (mwind_hbm, mwind_ref),
                (target_hbm, target_ref),
            )
        )
    ]
    for copy in inputs:
        copy.start()

    winds[...] = jnp.zeros_like(winds)
    halo[...] = jnp.zeros_like(halo)
    ghalo[...] = jnp.zeros_like(ghalo)
    barrier = pltpu.get_barrier_semaphore()
    greeted = 0
    for delta in (1, bands - 1, 2, bands - 2):
        pl.semaphore_signal(
            barrier, inc=1, device_id=band_device((band + delta) % bands), device_id_type=MESH
        )
        greeted += 1
    for d in range(1, levs):
        pl.semaphore_signal(
            barrier, inc=1, device_id=lev_device((lev + d) % levs), device_id_type=MESH
        )
        greeted += 1
    for d in range(1, side_y):
        pl.semaphore_signal(
            barrier, inc=1, device_id=y_device((my_y + d) % side_y), device_id_type=MESH
        )
        greeted += 1
    for d in range(1, side_z):
        pl.semaphore_signal(
            barrier, inc=1, device_id=z_device((my_z + d) % side_z), device_id_type=MESH
        )
        greeted += 1

    def prepare(net):
        w1 = w1_ref[:, net, :]
        b1 = b1_ref[net : net + 1, :]
        rows = jnp.concatenate([w1, b1, jnp.zeros((11, WIDTH), F32)], 0)
        hi, lo = split(rows)
        hi, lo = hi.astype(F32), lo.astype(F32)
        w1s[net] = jnp.concatenate([hi, hi, lo, jnp.zeros_like(hi)], 0).T.astype(BF16)
        hi, lo = split(rows[0:16])
        w1b[net, 0:16, 0:128] = hi
        w1b[net, 0:16, 128:256] = hi
        w1b[net, 16:32, 0:128] = lo
        w1b[net, 16:32, 128:256] = lo
        w2 = w2_ref[net]
        for ref, mat in ((w2s, w2.T), (w2b, w2)):
            hi, lo = split(mat)
            ref[net, 0:128, 0:128] = hi
            ref[net, 0:128, 128:256] = hi
            ref[net, 128:256, 0:128] = lo
            ref[net, 128:256, 128:256] = lo
        b2s[net] = jnp.broadcast_to(b2_ref[net : net + 1, :], (WIDTH, WIDTH)).T
        w3 = w3_ref[net]
        w3 = w3 - jnp.mean(w3, 0, keepdims=True)
        group = lax.broadcasted_iota(jnp.int32, (16, WIDTH), 0) // 4
        rep = jnp.zeros((16, WIDTH), F32)
        for j in range(4):
            rep = jnp.where(group == j, w3[j : j + 1, :], rep)
        hi, lo = split(rep)
        w3s[net, 0:16, 0:128] = hi
        w3s[net, 0:16, 128:256] = hi
        w3s[net, 16:32, 0:128] = lo
        w3s[net, 16:32, 128:256] = lo
        hi, lo = hi.astype(F32), lo.astype(F32)
        w3e[net] = jnp.concatenate([hi, hi, lo, jnp.zeros((80, WIDTH), F32)], 0).T.astype(BF16)
        b3 = b3_ref[net : net + 1, :]
        b3 = b3 - jnp.mean(b3, 1, keepdims=True)
        mine = (
            lax.broadcasted_iota(jnp.int32, (16, 4), 0) // 4
            == lax.broadcasted_iota(jnp.int32, (16, 4), 1)
        )
        column = jnp.sum(jnp.where(mine, b3, 0.0), 1, keepdims=True)
        place = lax.broadcasted_iota(jnp.int32, (16, WIDTH), 0) // 4
        base = jnp.where((place == 0) | (place == 3), BASE[0], BASE[1])
        b3s[net] = column + base

    def constant_rows(ref, lo_lane, courant, low, high):
        n = courant.shape[1]
        place = lax.broadcasted_iota(jnp.int32, (16, n), 0)
        rows = jnp.where(place == 0, courant, 0.0)
        rows = jnp.where(place == 1, courant * courant, rows)
        rows = jnp.where(place == 2, low, rows)
        rows = jnp.where(place == 3, high, rows)
        rows = jnp.where(place == 4, 1.0, rows)
        hi, lo = split(rows)
        for s in range(STEPS):
            ref[s, 272:288, lo_lane : lo_lane + n] = hi
            ref[s, 304:320, lo_lane : lo_lane + n] = lo
            ref[s, 336:352, lo_lane : lo_lane + n] = hi

    def forward(net, s, lanes, stencil, courant, ax, h2, s1, s2, st, cf):
        hi, lo = split(stencil)
        ax[s, 256:272, lanes] = hi
        ax[s, 288:304, lanes] = lo
        ax[s, 320:336, lanes] = hi
        st[s, :, lanes] = stencil
        one = dot(w1s[net, :, 0:96], ax[s, 256:352, lanes])
        yield
        one = jnp.tanh(one)
        s1[s, :, lanes] = 1.0 - one * one
        pair = stack(one)
        ax[s, 0:256, lanes] = pair
        yield
        out = dot(w2s[net], pair)
        yield
        bias = b2s[net]
        n = out.shape[1]
        bias = jnp.concatenate([bias] * (n // WIDTH), 1)
        two = jnp.tanh(out[0:128] + out[128:256] + bias)
        s2[s, :, lanes] = 1.0 - two * two
        pair = stack(two)
        h2[s, :, lanes] = pair
        yield
        out = dot(w3s[net], pair)
        yield
        coef = out[0:16] + out[16:32] + jnp.concatenate([b3s[net]] * (n // WIDTH), 1)
        cf[s, :, lanes] = coef
        terms = coef * stencil
        half = terms[0:8] + terms[8:16]
        return courant * (half + turn(half))

    def backward(net, s, lanes, dflux, courant, d1, d2, pb, s1, s2, st, cf):
        dq = courant * dflux
        dq = jnp.concatenate([dq, dq], 0)
        weighted = dq * st[s, :, lanes]
        hi, lo = split(weighted)
        pb[0:16, lanes] = hi
        pb[16:32, lanes] = lo
        yield
        two = dot(w3e[net, :, 0:48], jnp.concatenate([hi, lo, hi], 0))
        yield
        two = two * s2[s, :, lanes]
        pair = stack(two)
        d2[:, lanes] = pair
        yield
        out = dot(w2b[net], pair)
        yield
        one = (out[0:128] + out[128:256]) * s1[s, :, lanes]
        pair = stack(one)
        d1[:, lanes] = pair
        yield
        out = dot(w1b[net], pair)
        yield
        return out[0:16] + out[16:32] + cf[s, :, lanes] * dq, weighted

    def quads(x, m, n):
        return (x[0:m, 0:n] + x[m : 2 * m, n : 2 * n]) + (x[0:m, n : 2 * n] + x[m : 2 * m, 0:n])

    def weight_grads(net, s, lanes, ax, h2, d1, d2, pb):
        out = dot_nt(ax[s, 0:288, lanes], d2[:, lanes])
        acc2[net] += quads(out, 128, 128)
        accb2[net] += out[256:288, 0:128] + out[256:288, 128:256]
        out = dot_nt(ax[s, 256:320, lanes], d1[:, lanes])
        acc1[net] += quads(out, 32, 128)
        out = dot_nt(pb[:, lanes], h2[s, :, lanes])
        acc3[net] += quads(out, 16, 128)

    def lane_fold(x):
        out = x[:, 0:128]
        for i in range(1, x.shape[1] // 128):
            out = out + x[:, 128 * i : 128 * (i + 1)]
        return out

    zchunks = (slice(0, 256), slice(256, 512), slice(512, 640))

    def zonal_stencil():
        c = line[...]
        return jnp.concatenate(
            [pick(lane_roll(c, 1), c), pick(lane_roll(c, -1), lane_roll(c, -2))], 0
        )

    def zonal(s):
        stencil = zonal_stencil()
        parts = run(
            [
                forward(
                    0, s, lanes, stencil[:, lanes], zcour[:, lanes], ax_z, h2_z, s1_z, s2_z, st_z, cf_z
                )
                for lanes in zchunks
            ]
        )
        flux = jnp.concatenate(parts, 1)
        new = line[...] - (flux - lane_roll(flux, 1))
        halo[s, 2] = pick(*from_line(new))

    def face_stencil(s, face):
        mid = turn(halo[s, 2])
        if face == 1:
            return jnp.concatenate([halo[s, 1], halo[s, 2]], 0)
        if face == 3:
            return jnp.concatenate([halo[s, 2], halo[s, 3]], 0)
        if face == 2:
            return jnp.concatenate([pick(turn(halo[s, 1]), mid), pick(mid, turn(halo[s, 3]))], 0)
        if face == 0:
            before = turn(halo[s, 1])
            return jnp.concatenate([pick(turn(halo[s, 0]), before), pick(before, mid)], 0)
        after = turn(halo[s, 3])
        return jnp.concatenate([pick(mid, after), pick(after, turn(halo[s, 4]))], 0)

    def merid_faces(s, slots):
        fluxes = []
        for slot in slots:
            lanes = slice(slot * NY, (slot + 1) * NY)
            fluxes.append(
                forward(
                    1,
                    s,
                    lanes,
                    face_stencil(s, SLOT_FACE[slot]),
                    mcour[:, lanes],
                    ax_m,
                    h2_m,
                    s1_m,
                    s2_m,
                    st_m,
                    cf_m,
                )
            )
        return run(fluxes)

    def halo_copy(buf, s, which, send, recv):
        delta, slot = ((1, 1), (-1, 3), (2, 0), (-2, 4))[which]
        return pltpu.make_async_remote_copy(
            src_ref=buf.at[s, 2],
            dst_ref=buf.at[s, slot],
            send_sem=send.at[s, which],
            recv_sem=recv.at[s, which],
            device_id=band_device(band + delta),
            device_id_type=MESH,
        )

    has_target = (band < bands - 1, band >= 1, band < bands - 2, band >= 2)
    has_source = (band >= 1, band < bands - 1, band >= 2, band < bands - 2)

    def halo_start(buf, s, send, recv, which_all):
        for which in which_all:

            @pl.when(has_target[which])
            def _():
                halo_copy(buf, s, which, send, recv).start()

    def halo_wait(buf, s, send, recv, which_all):
        for which in which_all:

            @pl.when(has_source[which])
            def _():
                halo_copy(buf, s, which, send, recv).wait_recv()

    def halo_drain(buf, s, send, recv, which_all):
        for which in which_all:

            @pl.when(has_target[which])
            def _():
                halo_copy(buf, s, which, send, recv).wait_send()

    for copy in inputs:
        copy.wait()
    prepare(0)
    rows = [conc_ref[b, 0, r : r + 1, :] for r in range(2) for b in range(4)]
    line[...] = to_line(*both_rows(jnp.concatenate(rows, 0)))
    sea = sea_ref[...].astype(F32)
    zw = to_line(zwind_ref[0, 0:1, :], zwind_ref[0, 1:2, :])
    zs = to_line(sea[0:1, :], sea[1:2, :])
    courant = 0.5 * (zw + lane_roll(zw, -1))
    zcour[...] = jnp.broadcast_to(courant, (8, NZ))
    constant_rows(ax_z, 0, courant, zs, lane_roll(zs, -1))
    winds[0, 2, 0:2, :] = mwind_ref[0]
    winds[0, 2, 2:4, :] = sea
    for acc in (acc2, acc1, acc3, accb2, accp):
        acc[...] = jnp.zeros_like(acc)

    def forward_step(s, carry):
        zonal(s)

        @pl.when(s == 0)
        def _():
            pl.semaphore_wait(barrier, greeted)
            halo_start(winds, 0, wind_send, wind_recv, (0, 1))

        halo_start(halo, s, halo_send, halo_recv, (0, 1, 2, 3))

        @pl.when(s == 0)
        def _():
            prepare(1)
            halo_wait(winds, 0, wind_send, wind_recv, (0, 1))
            w = [winds[0, 1 + i // 2, i % 2 : i % 2 + 1, :] for i in range(6)]
            m = [winds[0, 1 + i // 2, 2 + i % 2 : 3 + i % 2, :] for i in range(6)]
            for slot, face in enumerate(SLOT_FACE):
                courant = 0.5 * (w[face] + w[face + 1])
                mcour[:, slot * NY : (slot + 1) * NY] = jnp.broadcast_to(courant, (8, NY))
                constant_rows(ax_m, slot * NY, courant, m[face], m[face + 1])

        @pl.when(s > 0)
        def _():
            halo_wait(halo, s - 1, halo_send, halo_recv, (2, 3))
            merid_faces(s - 1, (3, 4))

        halo_wait(halo, s, halo_send, halo_recv, (0, 1))
        f1, f2, f3 = merid_faces(s, (0, 1, 2))
        new = halo[s, 2] - pick(f2 - f1, f3 - f2)
        line[...] = to_line(*both_rows(new))

        @pl.when(s == STEPS - 1)
        def _():
            rows = [target_ref[b, 0, r : r + 1, :] for r in range(2) for b in range(4)]
            ghalo[STEPS - 1, 2] = (new - jnp.concatenate(rows, 0)) * loss_scale
            halo_start(ghalo, STEPS - 1, ghalo_send, ghalo_recv, (0, 1))
            for r in range(2):
                for b in range(4):
                    field_ref[b, 0, r : r + 1, :] = new[4 * r + b : 4 * r + b + 1, :]

        return carry

    lax.fori_loop(0, STEPS, forward_step, 0)
    halo_wait(halo, STEPS - 1, halo_send, halo_recv, (2, 3))
    merid_faces(STEPS - 1, (3, 4))

    def merid_back(s):
        halo_wait(ghalo, s, ghalo_send, ghalo_recv, (0, 1))
        g = []
        for block in (1, 2, 3):
            g.extend(both_rows(ghalo[s, block]))
        lows, highs = [None] * 5, [None] * 5
        first = None
        inner = None
        parts = []
        for slot, face in enumerate(SLOT_FACE):
            lanes = slice(slot * NY, (slot + 1) * NY)
            part = backward(
                1,
                s,
                lanes,
                g[face + 1] - g[face],
                mcour[:, lanes],
                d1_m,
                d2_m,
                pb_m,
                s1_m,
                s2_m,
                st_m,
                cf_m,
            )
            parts.append(part)
        for slot, (out, weighted) in enumerate(run(parts)):
            face = SLOT_FACE[slot]
            lows[face], highs[face] = out[0:8], out[8:16]
            if slot == 0:
                first = lane_fold(weighted)
            elif slot == 1:
                inner = lane_fold(weighted)
            elif slot == 2:
                inner = inner + lane_fold(weighted)
        new = ghalo[s, 2] + (highs[1] + lows[3])
        new = new + turn(pick(highs[2] + lows[4], highs[0] + lows[2]))
        accp[1] += inner

        @pl.when(band == 0)
        def _():
            accp[1] += first

        gline[...] = to_line(*both_rows(new))

    def zonal_back(s):
        gz = gline[...]
        dflux = lane_roll(gz, -1) - gz
        outs = run(
            [
                backward(
                    0,
                    s,
                    lanes,
                    dflux[:, lanes],
                    zcour[:, lanes],
                    d1_z,
                    d2_z,
                    pb_z,
                    s1_z,
                    s2_z,
                    st_z,
                    cf_z,
                )
                for lanes in zchunks
            ]
        )
        out = jnp.concatenate([o[0] for o in outs], 1)
        low, high = out[0:8], out[8:16]
        t = pick(lane_roll(low, -1), low) + pick(lane_roll(high, 1), lane_roll(high, 2))
        new = gz + t + turn(t)

        accp[0] += sum(lane_fold(o[1]) for o in outs)
        return pick(*from_line(new))

    def merid_weights(s):
        weight_grads(1, s, slice(NY, 3 * NY), ax_m, h2_m, d1_m, d2_m, pb_m)

        @pl.when(band == 0)
        def _():
            weight_grads(1, s, slice(0, NY), ax_m, h2_m, d1_m, d2_m, pb_m)

    def zonal_weights(s):
        weight_grads(0, s, slice(0, NZ), ax_z, h2_z, d1_z, d2_z, pb_z)

    def backward_step(i, carry):
        s = STEPS - 1 - i
        merid_back(s)
        ghalo[s - 1, 2] = zonal_back(s)
        halo_start(ghalo, s - 1, ghalo_send, ghalo_recv, (0, 1))
        merid_weights(s)
        zonal_weights(s)
        return carry

    lax.fori_loop(0, STEPS - 1, backward_step, 0)

    centre = jnp.where(
        lax.broadcasted_iota(jnp.int32, (16, 16), 1) // 4
        == lax.broadcasted_iota(jnp.int32, (16, 16), 0),
        0.75,
        -0.25,
    )
    centre = jnp.concatenate([centre, centre], 1).astype(BF16)

    def gather_net(net):
        top = net * NET_ROWS
        grads[top : top + 128] = acc2[net]
        grads[top + 128 : top + 160] = acc1[net]
        grads[top + 149 : top + 150] = accb2[net, 20:21, :]
        grads[top + 152 : top + 156] = dot(centre, stack(acc3[net]))[0:4]
        sums = jnp.sum(accp[net], 1, keepdims=True)
        mine = (
            lax.broadcasted_iota(jnp.int32, (16, WIDTH), 0) // 4
            == lax.broadcasted_iota(jnp.int32, (16, WIDTH), 1)
        )
        row = jnp.sum(jnp.where(mine, sums, 0.0), 0, keepdims=True)
        grads[top + 156 : top + 157] = row - jnp.sum(row, 1, keepdims=True) * 0.25

    piece = GRAD_ROWS // levs
    part = piece // side_y
    started = []

    def send(src, dst, index, device):
        copy = pltpu.make_async_remote_copy(
            src_ref=src,
            dst_ref=dst,
            send_sem=red_send.at[index],
            recv_sem=red_recv.at[index],
            device_id=device,
            device_id_type=MESH,
        )
        copy.start()
        started.append(copy)
        return copy

    def wait(copies):
        for copy in copies:
            copy.wait_recv()

    wide = levs // 2
    core = lev % 2
    my_x = lev // 2

    def first_copy(net, k):
        tx = (my_x + k) % wide
        slot = 2 * k + core
        row = pl.multiple_of(net * NET_ROWS + tx * piece, 8)
        return pltpu.make_async_remote_copy(
            src_ref=grads.at[pl.ds(row, piece)],
            dst_ref=r1.at[slot],
            send_sem=first_send.at[net, k],
            recv_sem=first_recv.at[slot],
            device_id=lev_device(2 * tx + net),
            device_id_type=MESH,
        )

    def send_net(net):
        for k in range(wide - 1, 0, -1):
            first_copy(net, k).start()

        @pl.when(core != net)
        def _():
            first_copy(net, 0).start()

    def drain_net(net):
        for k in range(1, wide):
            first_copy(net, k).wait_send()

        @pl.when(core != net)
        def _():
            first_copy(net, 0).wait_send()

    def arrived(slot):
        pltpu.make_async_copy(r1.at[slot], r1.at[slot], first_recv.at[slot]).wait()
        return r1[slot]

    merid_back(0)
    merid_weights(0)
    gather_net(1)
    send_net(1)
    zonal_back(0)
    zonal_weights(0)
    gather_net(0)
    send_net(0)
    row = pl.multiple_of(core * NET_ROWS + my_x * piece, 8)
    total = grads[pl.ds(row, piece)] + arrived(1 - core)
    for k in range(1, wide):
        for c in range(2):
            total = total + arrived(2 * k + c)
    at = 0
    for i in range(side_y):
        s1buf[i] = total[i * part : (i + 1) * part]
    copies = []
    for d in range(1, side_y):
        ty = (my_y + d) % side_y
        copies.append(send(s1buf.at[ty], r2.at[d - 1], at, y_device(ty)))
        at += 1
    total = s1buf[my_y]
    wait(copies)
    for d in range(1, side_y):
        total = total + r2[d - 1]
    r3[my_z] = total
    copies = []
    for d in range(1, side_z):
        tz = (my_z + d) % side_z
        copies.append(send(r3.at[my_z], r3.at[my_z], at, z_device(tz)))
        at += 1
    wait(copies)
    total = r3[0]
    for i in range(1, side_z):
        total = total + r3[i]
    a4[my_y] = total
    copies = []
    for d in range(1, side_y):
        ty = (my_y + d) % side_y
        copies.append(send(a4.at[my_y], a4.at[my_y], at, y_device(ty)))
        at += 1
    wait(copies)
    for i in range(side_y):
        full[lev, i * part : (i + 1) * part] = a4[i]
    copies = []
    for d in range(1, levs):
        tl = (lev + d) % levs
        copies.append(send(full.at[lev], full.at[lev], at, lev_device(tl)))
        at += 1
    wait(copies)
    for net in range(2):
        everything = jnp.concatenate([full[2 * x + net] for x in range(wide)], 0)
        top = 0
        gw2_ref[net] = everything[top : top + 128]
        gw1_ref[:, net, :] = everything[top + 128 : top + 148]
        gb1_ref[net : net + 1] = everything[top + 148 : top + 149]
        gb2_ref[net : net + 1] = everything[top + 149 : top + 150]
        gw3_ref[net] = everything[top + 152 : top + 156]
        gb3_ref[net : net + 1] = everything[top + 156 : top + 157, 0:4]

    for copy in started:
        copy.wait_send()
    drain_net(0)
    drain_net(1)
    halo_drain(winds, 0, wind_send, wind_recv, (0, 1))
    for s in range(STEPS):
        halo_drain(halo, s, halo_send, halo_recv, (0, 1, 2, 3))
        halo_drain(ghalo, s, ghalo_send, ghalo_recv, (0, 1))


def on_device(bands, levs, loss_scale, *args):
    piece = GRAD_ROWS // levs
    side_y = math.isqrt(bands)
    side_z = bands // side_y
    part = piece // side_y
    reductions = (levs - 1) + 2 * (side_y - 1) + (side_z - 1)
    vmem = pltpu.VMEM
    sweeps = [NZ, NM]
    args = list(args)
    args[5] = jnp.transpose(args[5], (1, 0, 2))
    scratch = [
        *[vmem(arg.shape, arg.dtype) for arg in args],
        pltpu.SemaphoreType.DMA((len(args),)),
        vmem((2, 128, 128), BF16),
        vmem((2, 256, 256), BF16),
        vmem((2, 32, 256), BF16),
        vmem((2, 128, 128), BF16),
        vmem((2, 256, 256), BF16),
        vmem((2, 32, 256), BF16),
        vmem((2, 128, 128), F32),
        vmem((2, 16, 128), F32),
        vmem((8, NZ), F32),
        vmem((8, NM), F32),
        vmem((STEPS, 5, 8, NY), F32),
        vmem((STEPS, 5, 8, NY), F32),
        vmem((1, 5, 8, NY), F32),
        vmem((8, NZ), F32),
        vmem((8, NZ), F32),
        *[vmem((STEPS, 352, n), BF16) for n in sweeps],
        *[vmem((STEPS, 256, n), BF16) for n in sweeps],
        *[vmem((STEPS, 128, n), F32) for n in sweeps],
        *[vmem((STEPS, 128, n), F32) for n in sweeps],
        *[vmem((STEPS, 16, n), F32) for n in sweeps],
        *[vmem((STEPS, 16, n), F32) for n in sweeps],
        *[vmem((256, n), BF16) for n in sweeps],
        *[vmem((256, n), BF16) for n in sweeps],
        *[vmem((32, n), BF16) for n in sweeps],
        vmem((2, 128, 128), F32),
        vmem((2, 32, 128), F32),
        vmem((2, 16, 128), F32),
        vmem((2, 32, 128), F32),
        vmem((2, 16, 128), F32),
        vmem((GRAD_ROWS, 128), F32),
        vmem((levs, piece, 128), F32),
        vmem((side_y, part, 128), F32),
        vmem((side_y - 1, part, 128), F32),
        vmem((side_z, part, 128), F32),
        vmem((side_y, part, 128), F32),
        vmem((levs, piece, 128), F32),
        pltpu.SemaphoreType.DMA((STEPS, 4)),
        pltpu.SemaphoreType.DMA((STEPS, 4)),
        pltpu.SemaphoreType.DMA((STEPS, 4)),
        pltpu.SemaphoreType.DMA((STEPS, 4)),
        pltpu.SemaphoreType.DMA((1, 4)),
        pltpu.SemaphoreType.DMA((1, 4)),
        pltpu.SemaphoreType.DMA((reductions,)),
        pltpu.SemaphoreType.DMA((reductions,)),
        pltpu.SemaphoreType.DMA((2, levs // 2)),
        pltpu.SemaphoreType.DMA((levs,)),
    ]
    out_shape = [jax.ShapeDtypeStruct(args[0].shape, F32)] + [
        jax.ShapeDtypeStruct(args[i].shape, F32) for i in range(5, 11)
    ]
    results = pl.pallas_call(
        functools.partial(kernel, bands, levs, loss_scale),
        out_shape=out_shape,
        in_specs=[pl.BlockSpec(memory_space=pltpu.HBM)] * 11,
        out_specs=[pl.BlockSpec(memory_space=pltpu.VMEM)] * 7,
        scratch_shapes=scratch,
        compiler_params=pltpu.CompilerParams(
            collective_id=0, has_side_effects=True, vmem_limit_bytes=48 * 1024 * 1024
        ),
        name="advection_step",
    )(*[pltpu.with_memory_space_constraint(arg, pltpu.HBM) for arg in args])
    results = list(
        pl.pallas_call(
            write_out,
            out_shape=out_shape,
            in_specs=[pl.BlockSpec(memory_space=pltpu.VMEM)] * 7,
            out_specs=[pl.BlockSpec(memory_space=pltpu.HBM)] * 7,
            scratch_shapes=[pltpu.SemaphoreType.DMA((7,))],
            compiler_params=pltpu.CompilerParams(vmem_limit_bytes=1024 * 1024),
            name="write_out",
        )(*results)
    )
    results[1] = jnp.transpose(results[1], (1, 0, 2))
    return tuple(results)


def write_out(*refs):
    sem = refs[14]
    copies = [pltpu.make_async_copy(refs[i], refs[7 + i], sem.at[i]) for i in range(7)]
    for copy in copies:
        copy.start()
    for copy in copies:
        copy.wait()


def solution(mesh):
    bands, levs = mesh.shape["band"], mesh.shape["lev"]
    loss_scale = 1.0 / math.sqrt(4 * levs * 2 * bands * NY)
    return jax.shard_map(
        functools.partial(on_device, bands, levs, loss_scale),
        mesh=mesh,
        in_specs=(
            P(None, "lev", "band", None),
            P(None, "lev", "band", None),
            P("lev", "band", None),
            P("lev", "band", None),
            P("band", None),
            P(),
            P(),
            P(),
            P(),
            P(),
            P(),
        ),
        out_specs=(P(None, "lev", "band", None), P(), P(), P(), P(), P(), P()),
        check_vma=False,
    )
```

```python
import contextlib
import functools
import math

import jax
import jax.numpy as jnp
from jax import lax
from jax.experimental import pallas as pl
from jax.experimental.pallas import tpu as pltpu
from jax.sharding import PartitionSpec as P

STEPS = 3
WIDTH = 128
F32 = jnp.float32
BF16 = jnp.bfloat16
LOGICAL = pl.DeviceIdType.LOGICAL
BASE = (-1.0 / 12.0, 7.0 / 12.0, 7.0 / 12.0, -1.0 / 12.0)

NY = 256
GAP = 64
NZ = 640
SLOT_FACE = (1, 2, 3, 0, 4)
NM = 5 * NY
NET_ROWS = 160
GRAD_ROWS = 2 * NET_ROWS


def mark(name):
    return contextlib.nullcontext()


def split(x):
    hi = x.astype(BF16)
    lo = (x - hi.astype(F32)).astype(BF16)
    return hi, lo


def stack(x):
    return jnp.concatenate(split(x), axis=0)


def dot(a, b):
    return lax.dot_general(a, b, (((1,), (0,)), ((), ())), preferred_element_type=F32)


def dot_nt(a, b):
    return lax.dot_general(a, b, (((1,), (1,)), ((), ())), preferred_element_type=F32)


def run(parts, skew=0):
    results = [None] * len(parts)
    live = set(range(len(parts)))
    tick = 0
    while live:
        for i in sorted(live):
            if tick >= i * skew:
                try:
                    next(parts[i])
                except StopIteration as stop:
                    results[i] = stop.value
                    live.discard(i)
        tick += 1
    return results


def far_first(n):
    return sorted(range(1, n), key=lambda d: -min(d, n - d))


def low_half(shape):
    return lax.broadcasted_iota(jnp.int32, shape, 0) < 4


def pick(a, b):
    return jnp.where(low_half(a.shape), a, b)


def turn(x):
    return pltpu.roll(x, 4, axis=0)


def lane_roll(x, shift):
    return pltpu.roll(x, shift % x.shape[1], axis=1)


def both_rows(block):
    turned = turn(block)
    return pick(block, turned), pick(turned, block)


def to_line(first, second):
    gap = jnp.zeros((first.shape[0], 2 * GAP), F32)
    return jnp.concatenate([lane_roll(jnp.concatenate([first, gap], 1), GAP), second], 1)


def from_line(line):
    return lane_roll(line[:, : NY + 2 * GAP], -GAP)[:, :NY], line[:, NY + 2 * GAP :]


def kernel(
    bands,
    levs,
    loss_scale,
    conc_hbm,
    target_hbm,
    zwind_hbm,
    mwind_hbm,
    sea_hbm,
    w1_hbm,
    b1_hbm,
    w2_hbm,
    b2_hbm,
    w3_hbm,
    b3_hbm,
    field_ref,
    gw1_ref,
    gb1_ref,
    gw2_ref,
    gb2_ref,
    gw3_ref,
    gb3_ref,
    conc_ref,
    target_ref,
    zwind_ref,
    mwind_ref,
    sea_ref,
    w1_ref,
    b1_ref,
    w2_ref,
    b2_ref,
    w3_ref,
    b3_ref,
    input_sem,
    w1s,
    w2s,
    w3s,
    w3e,
    w2b,
    w1b,
    b2s,
    b3s,
    zcour,
    mcour,
    halo,
    ghalo,
    winds,
    block_out,
    wind_out,
    pair_out,
    pair_in,
    final_out,
    final_in,
    line,
    gline,
    ax_z,
    ax_m,
    h2_z,
    h2_m,
    s1_z,
    s1_m,
    s2_z,
    s2_m,
    st_z,
    st_m,
    cf_z,
    cf_m,
    d1_z,
    d1_m,
    d2_z,
    d2_m,
    pb_z,
    pb_m,
    acc3,
    accb2,
    accp,
    grads,
    r1,
    s1buf,
    r2,
    r3,
    a4,
    full,
    halo_send,
    halo_recv,
    ghalo_send,
    ghalo_recv,
    wind_send,
    wind_recv,
    swap_send,
    swap_recv,
    red_send,
    red_recv,
):
    side_y = math.isqrt(bands)
    side_z = bands // side_y
    band = lax.axis_index("band")
    lev = lax.axis_index("lev")
    my_y = lax.div(band, side_z)
    my_z = lax.rem(band, side_z)

    def place(b):
        y = lax.div(b, side_z)
        z = b - y * side_z
        return b + lax.rem(y, 2) * (side_z - 1 - 2 * z)

    mine = place(band)
    moved = mine != band

    def wrap(at, n):
        return jnp.where(at >= n, at - n, at)

    def y_device(ty):
        return (ty * side_z + my_z) * levs + lev

    def z_device(tz):
        return (my_y * side_z + tz) * levs + lev

    def lev_device(tl):
        return band * levs + tl

    def band_device(tb):
        return tb * levs + lev

    inputs = [
        pltpu.make_async_copy(src, dst, input_sem.at[i])
        for i, (src, dst) in enumerate(
            (
                (w2_hbm, w2_ref),
                (w1_hbm, w1_ref),
                (b1_hbm, b1_ref),
                (b2_hbm, b2_ref),
                (w3_hbm, w3_ref),
                (b3_hbm, b3_ref),
                (conc_hbm, conc_ref),
                (zwind_hbm, zwind_ref),
                (sea_hbm, sea_ref),
                (mwind_hbm, mwind_ref),
                (target_hbm, target_ref),
            )
        )
    ]
    for copy in inputs:
        copy.start()

    winds[...] = jnp.zeros_like(winds)
    halo[...] = jnp.zeros_like(halo)
    ghalo[...] = jnp.zeros_like(ghalo)
    barrier = pltpu.get_barrier_semaphore()
    greeted = 0
    for d in range(1, levs):
        pl.semaphore_signal(
            barrier, inc=1, device_id=lev_device(wrap(lev + d, levs)), device_id_type=LOGICAL
        )
        greeted += 1
    for d in range(1, side_y):
        pl.semaphore_signal(
            barrier, inc=1, device_id=y_device(wrap(my_y + d, side_y)), device_id_type=LOGICAL
        )
        greeted += 1
    for d in range(1, side_z):
        pl.semaphore_signal(
            barrier, inc=1, device_id=z_device(wrap(my_z + d, side_z)), device_id_type=LOGICAL
        )
        greeted += 1

    near_end = (my_z < 2) | (my_z >= side_z - 2)

    def others():
        for delta in (1, -1, 2, -2):
            for base, mapped in ((band, True), (mine, False), (mine, True)):
                at = base + delta
                known = (at >= 0) & (at < bands)
                at = jnp.clip(at, 0, bands - 1)
                device = place(at) if mapped else at
                yield device, near_end & known & (lax.div(device, side_z) != my_y)

    @pl.when(near_end)
    def _():
        for device, other in others():

            @pl.when(other)
            def _():
                pl.semaphore_signal(
                    barrier, inc=1, device_id=band_device(device), device_id_type=LOGICAL
                )

    for _, other in others():
        greeted = greeted + other.astype(jnp.int32)

    def prepare(net):
        w1 = w1_ref[:, net, :]
        b1 = b1_ref[net : net + 1, :]
        rows = jnp.concatenate([w1, b1, jnp.zeros((11, WIDTH), F32)], 0)
        hi, lo = split(rows)
        hi, lo = hi.astype(F32), lo.astype(F32)
        w1s[net] = jnp.concatenate([hi, hi, lo, jnp.zeros_like(hi)], 0).T.astype(BF16)
        hi, lo = split(rows[0:16])
        w1b[net, 0:16, 0:128] = hi
        w1b[net, 0:16, 128:256] = hi
        w1b[net, 16:32, 0:128] = lo
        w1b[net, 16:32, 128:256] = lo
        w2 = w2_ref[net]
        for ref, mat in ((w2s, w2.T), (w2b, w2)):
            hi, lo = split(mat)
            ref[net, 0:128, 0:128] = hi
            ref[net, 0:128, 128:256] = hi
            ref[net, 128:256, 0:128] = lo
            ref[net, 128:256, 128:256] = lo
        b2s[net] = jnp.broadcast_to(b2_ref[net : net + 1, :], (WIDTH, WIDTH)).T
        w3 = w3_ref[net]
        w3 = w3 - jnp.mean(w3, 0, keepdims=True)
        group = lax.broadcasted_iota(jnp.int32, (16, WIDTH), 0) // 4
        rep = jnp.zeros((16, WIDTH), F32)
        for j in range(4):
            rep = jnp.where(group == j, w3[j : j + 1, :], rep)
        hi, lo = split(rep)
        w3s[net, 0:16, 0:128] = hi
        w3s[net, 0:16, 128:256] = hi
        w3s[net, 16:32, 0:128] = lo
        w3s[net, 16:32, 128:256] = lo
        hi, lo = hi.astype(F32), lo.astype(F32)
        w3e[net] = jnp.concatenate([hi, hi, lo, jnp.zeros((80, WIDTH), F32)], 0).T.astype(BF16)
        b3 = b3_ref[net : net + 1, :]
        b3 = b3 - jnp.mean(b3, 1, keepdims=True)
        mine = (
            lax.broadcasted_iota(jnp.int32, (16, 4), 0) // 4
            == lax.broadcasted_iota(jnp.int32, (16, 4), 1)
        )
        column = jnp.sum(jnp.where(mine, b3, 0.0), 1, keepdims=True)
        place = lax.broadcasted_iota(jnp.int32, (16, WIDTH), 0) // 4
        base = jnp.where((place == 0) | (place == 3), BASE[0], BASE[1])
        b3s[net] = column + base

    def constant_rows(ref, lo_lane, courant, low, high, steps):
        n = courant.shape[1]
        place = lax.broadcasted_iota(jnp.int32, (16, n), 0)
        rows = jnp.where(place == 0, courant, 0.0)
        rows = jnp.where(place == 1, courant * courant, rows)
        rows = jnp.where(place == 2, low, rows)
        rows = jnp.where(place == 3, high, rows)
        rows = jnp.where(place == 4, 1.0, rows)
        hi, lo = split(rows)
        for s in steps:
            ref[s, 272:288, lo_lane : lo_lane + n] = hi
            ref[s, 304:320, lo_lane : lo_lane + n] = lo
            ref[s, 336:352, lo_lane : lo_lane + n] = hi

    def forward(net, s, lanes, stencil, courant, ax, h2, s1, s2, st, cf):
        hi, lo = split(stencil)
        ax[s, 256:272, lanes] = hi
        ax[s, 288:304, lanes] = lo
        ax[s, 320:336, lanes] = hi
        st[s, :, lanes] = stencil
        one = dot(w1s[net, :, 0:96], ax[s, 256:352, lanes])
        yield
        one = jnp.tanh(one)
        s1[s, :, lanes] = 1.0 - one * one
        pair = stack(one)
        ax[s, 0:256, lanes] = pair
        yield
        out = dot(w2s[net], pair)
        yield
        bias = b2s[net]
        n = out.shape[1]
        bias = jnp.concatenate([bias] * (n // WIDTH), 1)
        two = jnp.tanh(out[0:128] + out[128:256] + bias)
        s2[s, :, lanes] = 1.0 - two * two
        pair = stack(two)
        h2[s, :, lanes] = pair
        yield
        out = dot(w3s[net], pair)
        yield
        coef = out[0:16] + out[16:32] + jnp.concatenate([b3s[net]] * (n // WIDTH), 1)
        cf[s, :, lanes] = coef
        terms = coef * stencil
        half = terms[0:8] + terms[8:16]
        return courant * (half + turn(half))

    def backward(net, s, lanes, dflux, courant, d1, d2, pb, s1, s2, st, cf, last=False):
        dq = courant * dflux
        dq = jnp.concatenate([dq, dq], 0)
        weighted = dq * st[s, :, lanes]
        hi, lo = split(weighted)
        pb[0:16, lanes] = hi
        pb[16:32, lanes] = lo
        yield
        two = dot(w3e[net, :, 0:48], jnp.concatenate([hi, lo, hi], 0))
        yield
        two = two * s2[s, :, lanes]
        pair = stack(two)
        d2[:, lanes] = pair
        yield
        out = dot(w2b[net], pair)
        yield
        one = (out[0:128] + out[128:256]) * s1[s, :, lanes]
        pair = stack(one)
        d1[:, lanes] = pair
        if last:
            return None, weighted
        yield
        out = dot(w1b[net], pair)
        yield
        return out[0:16] + out[16:32] + cf[s, :, lanes] * dq, weighted

    def quads(x, m, n):
        return (x[0:m, 0:n] + x[m : 2 * m, n : 2 * n]) + (x[0:m, n : 2 * n] + x[m : 2 * m, 0:n])

    def weight_grads(net, s, lanes, ax, h2, d1, d2, pb):
        out = dot_nt(ax[s, 0:288, lanes], d2[:, lanes])
        grads[net * NET_ROWS : net * NET_ROWS + 128] += quads(out, 128, 128)
        accb2[net] += out[256:288, 0:128] + out[256:288, 128:256]
        out = dot_nt(ax[s, 256:320, lanes], d1[:, lanes])
        grads[net * NET_ROWS + 128 : (net + 1) * NET_ROWS] += quads(out, 32, 128)
        out = dot_nt(pb[:, lanes], h2[s, :, lanes])
        acc3[net] += quads(out, 16, 128)

    def lane_fold(x):
        out = x[:, 0:128]
        for i in range(1, x.shape[1] // 128):
            out = out + x[:, 128 * i : 128 * (i + 1)]
        return out

    zchunks = (slice(0, 256), slice(256, 512), slice(512, 640))

    def zonal_stencil():
        c = line[...]
        return jnp.concatenate(
            [pick(lane_roll(c, 1), c), pick(lane_roll(c, -1), lane_roll(c, -2))], 0
        )

    def zonal(s):
        stencil = zonal_stencil()
        parts = run(
            [
                forward(
                    0, s, lanes, stencil[:, lanes], zcour[:, lanes], ax_z, h2_z, s1_z, s2_z, st_z, cf_z
                )
                for lanes in zchunks
            ]
        )
        flux = jnp.concatenate(parts, 1)
        new = line[...] - (flux - lane_roll(flux, 1))
        return pick(*from_line(new))

    def face_stencil(s, face):
        mid = turn(halo[s, 2])
        if face == 1:
            return jnp.concatenate([halo[s, 1], halo[s, 2]], 0)
        if face == 3:
            return jnp.concatenate([halo[s, 2], halo[s, 3]], 0)
        if face == 2:
            return jnp.concatenate([pick(turn(halo[s, 1]), mid), pick(mid, turn(halo[s, 3]))], 0)
        if face == 0:
            before = turn(halo[s, 1])
            return jnp.concatenate([pick(turn(halo[s, 0]), before), pick(before, mid)], 0)
        after = turn(halo[s, 3])
        return jnp.concatenate([pick(mid, after), pick(after, turn(halo[s, 4]))], 0)

    def merid_faces(s, slots):
        fluxes = []
        for slot in slots:
            lanes = slice(slot * NY, (slot + 1) * NY)
            fluxes.append(
                forward(
                    1,
                    s,
                    lanes,
                    face_stencil(s, SLOT_FACE[slot]),
                    mcour[:, lanes],
                    ax_m,
                    h2_m,
                    s1_m,
                    s2_m,
                    st_m,
                    cf_m,
                )
            )
        return run(fluxes)

    routes = ((1, 1), (-1, 3), (2, 0), (-2, 4))

    def inside(b):
        return (b >= 0) & (b < bands)

    def halo_copy(buf, s, which, send, recv):
        delta, slot = routes[which]
        return pltpu.make_async_remote_copy(
            src_ref=buf.at[s, 2],
            dst_ref=buf.at[s, slot],
            send_sem=send.at[which],
            recv_sem=recv.at[s, which],
            device_id=band_device(place(jnp.clip(mine + delta, 0, bands - 1))),
            device_id_type=LOGICAL,
        )

    def halo_start(buf, s, send, recv, which_all):
        for which in which_all:

            @pl.when(inside(mine + routes[which][0]))
            def _():
                halo_copy(buf, s, which, send, recv).start()

    def halo_wait(buf, s, send, recv, which_all):
        for which in which_all:

            @pl.when(inside(mine - routes[which][0]))
            def _():
                halo_copy(buf, s, which, send, recv).wait_recv()

    def halo_drain(buf, s, send, recv, which_all):
        for which in which_all:

            @pl.when(inside(mine + routes[which][0]))
            def _():
                halo_copy(buf, s, which, send, recv).wait_send()

    def move_copy(src, buf, which, send, recv):
        delta, slot = routes[which] if which < 4 else (0, 2)
        return pltpu.make_async_remote_copy(
            src_ref=src,
            dst_ref=buf.at[0, slot],
            send_sem=send.at[which],
            recv_sem=recv.at[0, which],
            device_id=band_device(place(jnp.clip(band + delta, 0, bands - 1))),
            device_id_type=LOGICAL,
        )

    def move_delta(which):
        return routes[which][0] if which < 4 else 0

    def move_start(src, buf, send, recv, which_all):
        for which in which_all:
            delta = move_delta(which)
            here = band + delta == mine

            @pl.when(inside(band + delta) & jnp.logical_not(here))
            def _():
                move_copy(src, buf, which, send, recv).start()

            @pl.when(here)
            def _():
                buf[0, routes[which][1] if which < 4 else 2] = src[...]

    def move_wait(src, buf, send, recv, which_all):
        for which in which_all:
            delta = move_delta(which)

            @pl.when(inside(mine - delta) & (mine - delta != band))
            def _():
                move_copy(src, buf, which, send, recv).wait_recv()

    def move_drain(src, buf, send, recv, which_all):
        for which in which_all:
            delta = move_delta(which)

            @pl.when(inside(band + delta) & (band + delta != mine))
            def _():
                move_copy(src, buf, which, send, recv).wait_send()

    def swap_copy(src, dst, index):
        return pltpu.make_async_remote_copy(
            src_ref=src,
            dst_ref=dst,
            send_sem=swap_send.at[index],
            recv_sem=swap_recv.at[index],
            device_id=band_device(mine),
            device_id_type=LOGICAL,
        )

    for copy in inputs:
        copy.wait()
    def block_of(ref):
        rows = [ref[b, 0, r : r + 1, :] for r in range(2) for b in range(4)]
        return jnp.concatenate(rows, 0)

    def zonal_constants(slab, steps):
        zw = to_line(slab[4:5, :], slab[5:6, :])
        zs = to_line(slab[2:3, :], slab[3:4, :])
        courant = 0.5 * (zw + lane_roll(zw, -1))
        zcour[...] = jnp.broadcast_to(courant, (8, NZ))
        constant_rows(ax_z, 0, courant, zs, lane_roll(zs, -1), steps)

    with mark("prepare"):
        prepare(0)
        pair_out[0] = block_of(conc_ref)
        pair_out[1] = block_of(target_ref)
        slab = jnp.concatenate(
            [mwind_ref[0], sea_ref[...].astype(F32), zwind_ref[0], zwind_ref[0]], 0
        )
        wind_out[...] = slab
        line[...] = to_line(*both_rows(pair_out[0]))
        zonal_constants(slab, range(STEPS))
        for acc in (grads, acc3, accb2, accp):
            acc[...] = jnp.zeros_like(acc)
    with mark("zonal"):
        block_out[...] = zonal(0)
    with mark("barrier"):
        pl.semaphore_wait(barrier, greeted)
    move_start(block_out, halo, halo_send, halo_recv, (0, 1, 4))
    move_start(wind_out, winds, wind_send, wind_recv, (0, 1, 4))
    move_start(block_out, halo, halo_send, halo_recv, (2, 3))

    @pl.when(moved)
    def _():
        swap_copy(pair_out, pair_in, 0).start()

    @pl.when(jnp.logical_not(moved))
    def _():
        pair_in[...] = pair_out[...]

    with mark("prepare1"):
        prepare(1)
    with mark("waitwind"):
        move_wait(wind_out, winds, wind_send, wind_recv, (0, 1, 4))
    with mark("constants"):
        w = [winds[0, 1 + i // 2, i % 2 : i % 2 + 1, :] for i in range(6)]
        m = [winds[0, 1 + i // 2, 2 + i % 2 : 3 + i % 2, :] for i in range(6)]
        for slot, face in enumerate(SLOT_FACE):
            courant = 0.5 * (w[face] + w[face + 1])
            mcour[:, slot * NY : (slot + 1) * NY] = jnp.broadcast_to(courant, (8, NY))
            constant_rows(ax_m, slot * NY, courant, m[face], m[face + 1], range(STEPS))

        @pl.when(moved)
        def _():
            zonal_constants(winds[0, 2], range(STEPS))

    with mark("waitmove"):
        move_wait(block_out, halo, halo_send, halo_recv, (0, 1, 4))

    def merid(s):
        with mark("merid"):
            f1, f2, f3 = merid_faces(s, (0, 1, 2))
            new = halo[s, 2] - pick(f2 - f1, f3 - f2)
            line[...] = to_line(*both_rows(new))
        return new

    move_drain(block_out, halo, halo_send, halo_recv, (0, 1, 2, 3, 4))
    merid(0)

    def forward_step(s, carry):
        with mark("zonal"):
            halo[s, 2] = zonal(s)
        halo_start(halo, s, halo_send, halo_recv, (0, 1, 2, 3))

        with mark("redundant"):

            @pl.when(s == 1)
            def _():
                move_wait(block_out, halo, halo_send, halo_recv, (2, 3))

            @pl.when(s > 1)
            def _():
                halo_wait(halo, s - 1, halo_send, halo_recv, (2, 3))

            merid_faces(s - 1, (3, 4))
        with mark("waithalo"):
            halo_wait(halo, s, halo_send, halo_recv, (0, 1))
        halo_drain(halo, s, halo_send, halo_recv, (0, 1, 2, 3))
        new = merid(s)

        @pl.when(s == STEPS - 1)
        def _():
            @pl.when(moved)
            def _():
                swap_copy(pair_out, pair_in, 0).wait_recv()

            ghalo[STEPS - 1, 2] = (new - pair_in[1]) * loss_scale
            halo_start(ghalo, STEPS - 1, ghalo_send, ghalo_recv, (0, 1))
            final_out[...] = new

            @pl.when(moved)
            def _():
                swap_copy(final_out, final_in, 1).start()

        return carry

    lax.fori_loop(1, STEPS, forward_step, 0)
    with mark("redundant"):
        halo_wait(halo, STEPS - 1, halo_send, halo_recv, (2, 3))
        merid_faces(STEPS - 1, (3, 4))

    @pl.when(moved)
    def _():
        with mark("zonal_again"):
            line[...] = to_line(*both_rows(pair_in[0]))
            zonal(0)

    def merid_back(s):
        with mark("waitg"):
            halo_wait(ghalo, s, ghalo_send, ghalo_recv, (0, 1))
        halo_drain(ghalo, s, ghalo_send, ghalo_recv, (0, 1))
        g = []
        for block in (1, 2, 3):
            g.extend(both_rows(ghalo[s, block]))
        lows, highs = [None] * 5, [None] * 5
        first = None
        inner = None
        parts = []
        for slot, face in enumerate(SLOT_FACE):
            lanes = slice(slot * NY, (slot + 1) * NY)
            part = backward(
                1,
                s,
                lanes,
                g[face + 1] - g[face],
                mcour[:, lanes],
                d1_m,
                d2_m,
                pb_m,
                s1_m,
                s2_m,
                st_m,
                cf_m,
            )
            parts.append(part)
        for slot, (out, weighted) in enumerate(run(parts)):
            face = SLOT_FACE[slot]
            lows[face], highs[face] = out[0:8], out[8:16]
            if slot == 0:
                first = lane_fold(weighted)
            elif slot == 1:
                inner = lane_fold(weighted)
            elif slot == 2:
                inner = inner + lane_fold(weighted)
        new = ghalo[s, 2] + (highs[1] + lows[3])
        new = new + turn(pick(highs[2] + lows[4], highs[0] + lows[2]))
        accp[1] += inner

        @pl.when(mine == 0)
        def _():
            accp[1] += first

        gline[...] = to_line(*both_rows(new))

    def zonal_back(s, last=False):
        gz = gline[...]
        dflux = lane_roll(gz, -1) - gz
        outs = run(
            [
                backward(
                    0,
                    s,
                    lanes,
                    dflux[:, lanes],
                    zcour[:, lanes],
                    d1_z,
                    d2_z,
                    pb_z,
                    s1_z,
                    s2_z,
                    st_z,
                    cf_z,
                    last,
                )
                for lanes in zchunks
            ]
        )
        accp[0] += sum(lane_fold(o[1]) for o in outs)
        if last:
            return None
        out = jnp.concatenate([o[0] for o in outs], 1)
        low, high = out[0:8], out[8:16]
        t = pick(lane_roll(low, -1), low) + pick(lane_roll(high, 1), lane_roll(high, 2))
        new = gz + t + turn(t)

        return pick(*from_line(new))

    def merid_weights(s):
        weight_grads(1, s, slice(NY, 3 * NY), ax_m, h2_m, d1_m, d2_m, pb_m)

        @pl.when(mine == 0)
        def _():
            weight_grads(1, s, slice(0, NY), ax_m, h2_m, d1_m, d2_m, pb_m)

    def zonal_weights(s):
        weight_grads(0, s, slice(0, NZ), ax_z, h2_z, d1_z, d2_z, pb_z)

    def backward_step(i, carry):
        s = STEPS - 1 - i
        merid_back(s)
        ghalo[s - 1, 2] = zonal_back(s)
        halo_start(ghalo, s - 1, ghalo_send, ghalo_recv, (0, 1))
        with mark("weights"):
            merid_weights(s)
            zonal_weights(s)
        return carry

    lax.fori_loop(0, STEPS - 1, backward_step, 0)

    centre = jnp.where(
        lax.broadcasted_iota(jnp.int32, (16, 16), 1) // 4
        == lax.broadcasted_iota(jnp.int32, (16, 16), 0),
        0.75,
        -0.25,
    )
    centre = jnp.concatenate([centre, centre], 1).astype(BF16)

    def gather_net(net):
        top = net * NET_ROWS
        grads[top + 149 : top + 150] = accb2[net, 20:21, :]
        grads[top + 152 : top + 156] = dot(centre, stack(acc3[net]))[0:4]
        sums = jnp.sum(accp[net], 1, keepdims=True)
        mine = (
            lax.broadcasted_iota(jnp.int32, (16, WIDTH), 0) // 4
            == lax.broadcasted_iota(jnp.int32, (16, WIDTH), 1)
        )
        row = jnp.sum(jnp.where(mine, sums, 0.0), 0, keepdims=True)
        grads[top + 156 : top + 157] = row - jnp.sum(row, 1, keepdims=True) * 0.25

    piece = GRAD_ROWS // levs
    part = piece // side_y
    started = []

    def send(src, dst, phase, device):
        pltpu.make_async_remote_copy(
            src_ref=src,
            dst_ref=dst,
            send_sem=red_send.at[phase],
            recv_sem=red_recv.at[phase],
            device_id=device,
            device_id_type=LOGICAL,
        ).start()

    def wait(buf, count, phase):
        with mark("wait_ar"):
            some = buf.at[0:count]
            pltpu.make_async_copy(some, some, red_recv.at[phase]).wait()
        started.append((some, phase))

    wide = levs // 2
    my_x = lax.div(lev, 2)
    core = lev - 2 * my_x

    def first_copy(net, k):
        tx = wrap(my_x + k, wide)
        slot = 2 * k + core
        row = pl.multiple_of(net * NET_ROWS + tx * piece, 8)
        return pltpu.make_async_remote_copy(
            src_ref=grads.at[pl.ds(row, piece)],
            dst_ref=r1.at[slot],
            send_sem=red_send.at[0],
            recv_sem=red_recv.at[0],
            device_id=lev_device(2 * tx + net),
            device_id_type=LOGICAL,
        )

    def send_net(net):
        for k in far_first(wide):
            first_copy(net, k).start()

        @pl.when(core != net)
        def _():
            first_copy(net, 0).start()

    merid_back(0)
    with mark("wg1"):
        merid_weights(0)
    with mark("gather1"):
        gather_net(1)
        send_net(1)
    with mark("zback0"):
        zonal_back(0, True)
    with mark("wg0"):
        zonal_weights(0)
    with mark("gather0"):
        gather_net(0)
        send_net(0)
    @pl.when(moved)
    def _():
        swap_copy(final_out, final_in, 1).wait()
        swap_copy(pair_out, pair_in, 0).wait_send()

    final = jnp.where(moved, final_in[...], final_out[...])
    for r in range(2):
        for b in range(4):
            field_ref[b, 0, r : r + 1, :] = final[4 * r + b : 4 * r + b + 1, :]
    move_drain(wind_out, winds, wind_send, wind_recv, (0, 1, 4))

    row = pl.multiple_of(core * NET_ROWS + my_x * piece, 8)
    with mark("wait_ar"):
        wait(r1, levs - 1, 0)
        total = grads[pl.ds(row, piece)] + r1[1 - core]
        for k in range(1, wide):
            for c in range(2):
                total = total + r1[2 * k + c]
    for i in range(side_y):
        s1buf[i] = total[i * part : (i + 1) * part]
    for d in far_first(side_y):
        ty = wrap(my_y + d, side_y)
        send(s1buf.at[ty], r2.at[d - 1], 1, y_device(ty))
    total = s1buf[my_y]
    wait(r2, side_y - 1, 1)
    for d in range(1, side_y):
        total = total + r2[d - 1]
    r3[my_z] = total
    for d in far_first(side_z):
        tz = wrap(my_z + d, side_z)
        send(r3.at[my_z], r3.at[my_z], 2, z_device(tz))
    wait(r3, side_z - 1, 2)
    total = r3[0]
    for i in range(1, side_z):
        total = total + r3[i]
    a4[my_y] = total
    for d in far_first(side_y):
        ty = wrap(my_y + d, side_y)
        send(a4.at[my_y], a4.at[my_y], 3, y_device(ty))
    wait(a4, side_y - 1, 3)
    for i in range(side_y):
        full[lev, i * part : (i + 1) * part] = a4[i]
    for d in sorted(range(1, levs), key=lambda d: -min(d // 2, wide - d // 2)):
        tl = wrap(lev + d, levs)
        send(full.at[lev], full.at[lev], 4, lev_device(tl))
    wait(full, levs - 1, 4)
    for net in range(2):
        everything = jnp.concatenate([full[2 * x + net] for x in range(wide)], 0)
        top = 0
        gw2_ref[net] = everything[top : top + 128]
        gw1_ref[:, net, :] = everything[top + 128 : top + 148]
        gb1_ref[net : net + 1] = everything[top + 148 : top + 149]
        gb2_ref[net : net + 1] = everything[top + 149 : top + 150]
        gw3_ref[net] = everything[top + 152 : top + 156]
        gb3_ref[net : net + 1] = everything[top + 156 : top + 157, 0:4]

    for some, phase in started:
        pltpu.make_async_copy(some, some, red_send.at[phase]).wait()


def on_device(bands, levs, loss_scale, *args):
    piece = GRAD_ROWS // levs
    side_y = math.isqrt(bands)
    side_z = bands // side_y
    part = piece // side_y
    vmem = pltpu.VMEM
    sweeps = [NZ, NM]
    args = list(args)
    args[5] = jnp.transpose(args[5], (1, 0, 2))
    scratch = [
        *[vmem(arg.shape, arg.dtype) for arg in args],
        pltpu.SemaphoreType.DMA((len(args),)),
        vmem((2, 128, 128), BF16),
        vmem((2, 256, 256), BF16),
        vmem((2, 32, 256), BF16),
        vmem((2, 128, 128), BF16),
        vmem((2, 256, 256), BF16),
        vmem((2, 32, 256), BF16),
        vmem((2, 128, 128), F32),
        vmem((2, 16, 128), F32),
        vmem((8, NZ), F32),
        vmem((8, NM), F32),
        vmem((STEPS, 5, 8, NY), F32),
        vmem((STEPS, 5, 8, NY), F32),
        vmem((1, 5, 8, NY), F32),
        vmem((8, NY), F32),
        vmem((8, NY), F32),
        vmem((2, 8, NY), F32),
        vmem((2, 8, NY), F32),
        vmem((8, NY), F32),
        vmem((8, NY), F32),
        vmem((8, NZ), F32),
        vmem((8, NZ), F32),
        *[vmem((STEPS, 352, n), BF16) for n in sweeps],
        *[vmem((STEPS, 256, n), BF16) for n in sweeps],
        *[vmem((STEPS, 128, n), F32) for n in sweeps],
        *[vmem((STEPS, 128, n), F32) for n in sweeps],
        *[vmem((STEPS, 16, n), F32) for n in sweeps],
        *[vmem((STEPS, 16, n), F32) for n in sweeps],
        *[vmem((256, n), BF16) for n in sweeps],
        *[vmem((256, n), BF16) for n in sweeps],
        *[vmem((32, n), BF16) for n in sweeps],
        vmem((2, 16, 128), F32),
        vmem((2, 32, 128), F32),
        vmem((2, 16, 128), F32),
        vmem((GRAD_ROWS, 128), F32),
        vmem((levs, piece, 128), F32),
        vmem((side_y, part, 128), F32),
        vmem((side_y - 1, part, 128), F32),
        vmem((side_z, part, 128), F32),
        vmem((side_y, part, 128), F32),
        vmem((levs, piece, 128), F32),
        pltpu.SemaphoreType.DMA((5,)),
        pltpu.SemaphoreType.DMA((STEPS, 5)),
        pltpu.SemaphoreType.DMA((2,)),
        pltpu.SemaphoreType.DMA((STEPS, 2)),
        pltpu.SemaphoreType.DMA((5,)),
        pltpu.SemaphoreType.DMA((1, 5)),
        pltpu.SemaphoreType.DMA((2,)),
        pltpu.SemaphoreType.DMA((2,)),
        pltpu.SemaphoreType.DMA((5,)),
        pltpu.SemaphoreType.DMA((5,)),
    ]
    out_shape = [jax.ShapeDtypeStruct(args[0].shape, F32)] + [
        jax.ShapeDtypeStruct(args[i].shape, F32) for i in range(5, 11)
    ]
    results = pl.pallas_call(
        functools.partial(kernel, bands, levs, loss_scale),
        out_shape=out_shape,
        in_specs=[pl.BlockSpec(memory_space=pltpu.HBM)] * 11,
        out_specs=[pl.BlockSpec(memory_space=pltpu.VMEM)] * 7,
        scratch_shapes=scratch,
        compiler_params=pltpu.CompilerParams(
            collective_id=0, has_side_effects=True, vmem_limit_bytes=48 * 1024 * 1024
        ),
        name="advection_step",
    )(*[pltpu.with_memory_space_constraint(arg, pltpu.HBM) for arg in args])
    results = list(
        pl.pallas_call(
            write_out,
            out_shape=out_shape,
            in_specs=[pl.BlockSpec(memory_space=pltpu.VMEM)] * 7,
            out_specs=[pl.BlockSpec(memory_space=pltpu.HBM)] * 7,
            scratch_shapes=[pltpu.SemaphoreType.DMA((7,))],
            compiler_params=pltpu.CompilerParams(vmem_limit_bytes=1024 * 1024),
            name="write_out",
        )(*results)
    )
    results[1] = jnp.transpose(results[1], (1, 0, 2))
    return tuple(results)


def write_out(*refs):
    sem = refs[14]
    copies = [pltpu.make_async_copy(refs[i], refs[7 + i], sem.at[i]) for i in range(7)]
    for copy in copies:
        copy.start()
    for copy in copies:
        copy.wait()


def solution(mesh):
    bands, levs = mesh.shape["band"], mesh.shape["lev"]
    loss_scale = 1.0 / math.sqrt(4 * levs * 2 * bands * NY)
    return jax.shard_map(
        functools.partial(on_device, bands, levs, loss_scale),
        mesh=mesh,
        in_specs=(
            P(None, "lev", "band", None),
            P(None, "lev", "band", None),
            P("lev", "band", None),
            P("lev", "band", None),
            P("band", None),
            P(),
            P(),
            P(),
            P(),
            P(),
            P(),
        ),
        out_specs=(P(None, "lev", "band", None), P(), P(), P(), P(), P(), P()),
        check_vma=False,
    )
```

```python
import contextlib
import functools
import math

import jax
import jax.numpy as jnp
from jax import lax
from jax.experimental import pallas as pl
from jax.experimental.pallas import tpu as pltpu
from jax.sharding import PartitionSpec as P

STEPS = 3
WIDTH = 128
F32 = jnp.float32
BF16 = jnp.bfloat16
LOGICAL = pl.DeviceIdType.LOGICAL
BASE = (-1.0 / 12.0, 7.0 / 12.0, 7.0 / 12.0, -1.0 / 12.0)

NY = 256
GAP = 64
NZ = 640
SLOT_FACE = (1, 2, 3, 0, 4, -1, 5)
NM = 7 * NY
NB = 5 * NY
NET_ROWS = 160
GRAD_ROWS = 2 * NET_ROWS


def mark(name):
    return contextlib.nullcontext()


def split(x):
    hi = x.astype(BF16)
    lo = (x - hi.astype(F32)).astype(BF16)
    return hi, lo


def stack(x):
    return jnp.concatenate(split(x), axis=0)


def dot(a, b):
    return lax.dot_general(a, b, (((1,), (0,)), ((), ())), preferred_element_type=F32)


def dot_nt(a, b):
    return lax.dot_general(a, b, (((1,), (1,)), ((), ())), preferred_element_type=F32)


def run(parts, skew=0):
    results = [None] * len(parts)
    live = set(range(len(parts)))
    tick = 0
    while live:
        for i in sorted(live):
            if tick >= i * skew:
                try:
                    next(parts[i])
                except StopIteration as stop:
                    results[i] = stop.value
                    live.discard(i)
        tick += 1
    return results


def far_first(n):
    return sorted(range(1, n), key=lambda d: -min(d, n - d))


def low_half(shape):
    return lax.broadcasted_iota(jnp.int32, shape, 0) < 4


def pick(a, b):
    return jnp.where(low_half(a.shape), a, b)


def turn(x):
    return pltpu.roll(x, 4, axis=0)


def lane_roll(x, shift):
    return pltpu.roll(x, shift % x.shape[1], axis=1)


def both_rows(block):
    turned = turn(block)
    return pick(block, turned), pick(turned, block)


def to_line(first, second):
    gap = jnp.zeros((first.shape[0], 2 * GAP), F32)
    return jnp.concatenate([lane_roll(jnp.concatenate([first, gap], 1), GAP), second], 1)


def from_line(line):
    return lane_roll(line[:, : NY + 2 * GAP], -GAP)[:, :NY], line[:, NY + 2 * GAP :]


def kernel(
    bands,
    levs,
    loss_scale,
    conc_hbm,
    target_hbm,
    zwind_hbm,
    mwind_hbm,
    sea_hbm,
    w1_hbm,
    b1_hbm,
    w2_hbm,
    b2_hbm,
    w3_hbm,
    b3_hbm,
    field_ref,
    gw1_ref,
    gb1_ref,
    gw2_ref,
    gb2_ref,
    gw3_ref,
    gb3_ref,
    conc_ref,
    target_ref,
    zwind_ref,
    mwind_ref,
    sea_ref,
    w1_ref,
    b1_ref,
    w2_ref,
    b2_ref,
    w3_ref,
    b3_ref,
    input_sem,
    w1s,
    w2s,
    w3s,
    w3e,
    w2b,
    w1b,
    b2s,
    b3s,
    zcour,
    mcour,
    halo,
    ghalo,
    winds,
    block_out,
    wind_out,
    conc_out,
    conc_in,
    target_out,
    targets,
    final_out,
    final_in,
    line,
    gline,
    ax_z,
    ax_m,
    h2_z,
    h2_m,
    s1_z,
    s1_m,
    s2_z,
    s2_m,
    st_z,
    st_m,
    cf_z,
    cf_m,
    d1_z,
    d1_m,
    d2_z,
    d2_m,
    pb_z,
    pb_m,
    acc3,
    accb2,
    accp,
    grads,
    r1,
    s1buf,
    r2,
    r3,
    a4,
    full,
    halo_send,
    halo_recv,
    ghalo_send,
    ghalo_recv,
    wind_send,
    wind_recv,
    target_send,
    target_recv,
    swap_send,
    swap_recv,
    red_send,
    red_recv,
):
    side_y = math.isqrt(bands)
    side_z = bands // side_y
    band = lax.axis_index("band")
    lev = lax.axis_index("lev")
    my_y = lax.div(band, side_z)
    my_z = lax.rem(band, side_z)

    def place(b):
        y = lax.div(b, side_z)
        z = b - y * side_z
        return b + lax.rem(y, 2) * (side_z - 1 - 2 * z)

    mine = place(band)
    moved = mine != band

    def wrap(at, n):
        return jnp.where(at >= n, at - n, at)

    def y_device(ty):
        return (ty * side_z + my_z) * levs + lev

    def z_device(tz):
        return (my_y * side_z + tz) * levs + lev

    def lev_device(tl):
        return band * levs + tl

    def band_device(tb):
        return tb * levs + lev

    inputs = [
        pltpu.make_async_copy(src, dst, input_sem.at[i])
        for i, (src, dst) in enumerate(
            (
                (w2_hbm, w2_ref),
                (w1_hbm, w1_ref),
                (b1_hbm, b1_ref),
                (b2_hbm, b2_ref),
                (w3_hbm, w3_ref),
                (b3_hbm, b3_ref),
                (conc_hbm, conc_ref),
                (zwind_hbm, zwind_ref),
                (sea_hbm, sea_ref),
                (mwind_hbm, mwind_ref),
                (target_hbm, target_ref),
            )
        )
    ]
    for copy in inputs:
        copy.start()

    winds[...] = jnp.zeros_like(winds)
    halo[...] = jnp.zeros_like(halo)
    ghalo[...] = jnp.zeros_like(ghalo)
    targets[...] = jnp.zeros_like(targets)
    barrier = pltpu.get_barrier_semaphore()
    greeted = 0
    for d in range(1, levs):
        pl.semaphore_signal(
            barrier, inc=1, device_id=lev_device(wrap(lev + d, levs)), device_id_type=LOGICAL
        )
        greeted += 1
    for d in range(1, side_y):
        pl.semaphore_signal(
            barrier, inc=1, device_id=y_device(wrap(my_y + d, side_y)), device_id_type=LOGICAL
        )
        greeted += 1
    for d in range(1, side_z):
        pl.semaphore_signal(
            barrier, inc=1, device_id=z_device(wrap(my_z + d, side_z)), device_id_type=LOGICAL
        )
        greeted += 1

    near_end = (my_z < 2) | (my_z >= side_z - 2)

    def others():
        for delta in (1, -1, 2, -2):
            for base, mapped in ((band, True), (mine, False), (mine, True)):
                at = base + delta
                known = (at >= 0) & (at < bands)
                at = jnp.clip(at, 0, bands - 1)
                device = place(at) if mapped else at
                yield device, near_end & known & (lax.div(device, side_z) != my_y)

    @pl.when(near_end)
    def _():
        for device, other in others():

            @pl.when(other)
            def _():
                pl.semaphore_signal(
                    barrier, inc=1, device_id=band_device(device), device_id_type=LOGICAL
                )

    for _, other in others():
        greeted = greeted + other.astype(jnp.int32)

    def prepare(net):
        w1 = w1_ref[:, net, :]
        b1 = b1_ref[net : net + 1, :]
        rows = jnp.concatenate([w1, b1, jnp.zeros((11, WIDTH), F32)], 0)
        hi, lo = split(rows)
        hi, lo = hi.astype(F32), lo.astype(F32)
        w1s[net] = jnp.concatenate([hi, hi, lo, jnp.zeros_like(hi)], 0).T.astype(BF16)
        hi, lo = split(rows[0:16])
        w1b[net, 0:16, 0:128] = hi
        w1b[net, 0:16, 128:256] = hi
        w1b[net, 16:32, 0:128] = lo
        w1b[net, 16:32, 128:256] = lo
        w2 = w2_ref[net]
        for ref, mat in ((w2s, w2.T), (w2b, w2)):
            hi, lo = split(mat)
            ref[net, 0:128, 0:128] = hi
            ref[net, 0:128, 128:256] = hi
            ref[net, 128:256, 0:128] = lo
            ref[net, 128:256, 128:256] = lo
        b2s[net] = jnp.broadcast_to(b2_ref[net : net + 1, :], (WIDTH, WIDTH)).T
        w3 = w3_ref[net]
        w3 = w3 - jnp.mean(w3, 0, keepdims=True)
        group = lax.broadcasted_iota(jnp.int32, (16, WIDTH), 0) // 4
        rep = jnp.zeros((16, WIDTH), F32)
        for j in range(4):
            rep = jnp.where(group == j, w3[j : j + 1, :], rep)
        hi, lo = split(rep)
        w3s[net, 0:16, 0:128] = hi
        w3s[net, 0:16, 128:256] = hi
        w3s[net, 16:32, 0:128] = lo
        w3s[net, 16:32, 128:256] = lo
        hi, lo = hi.astype(F32), lo.astype(F32)
        w3e[net] = jnp.concatenate([hi, hi, lo, jnp.zeros((80, WIDTH), F32)], 0).T.astype(BF16)
        b3 = b3_ref[net : net + 1, :]
        b3 = b3 - jnp.mean(b3, 1, keepdims=True)
        mine = (
            lax.broadcasted_iota(jnp.int32, (16, 4), 0) // 4
            == lax.broadcasted_iota(jnp.int32, (16, 4), 1)
        )
        column = jnp.sum(jnp.where(mine, b3, 0.0), 1, keepdims=True)
        place = lax.broadcasted_iota(jnp.int32, (16, WIDTH), 0) // 4
        base = jnp.where((place == 0) | (place == 3), BASE[0], BASE[1])
        b3s[net] = column + base

    def constant_rows(ref, lo_lane, courant, low, high, steps):
        n = courant.shape[1]
        place = lax.broadcasted_iota(jnp.int32, (16, n), 0)
        rows = jnp.where(place == 0, courant, 0.0)
        rows = jnp.where(place == 1, courant * courant, rows)
        rows = jnp.where(place == 2, low, rows)
        rows = jnp.where(place == 3, high, rows)
        rows = jnp.where(place == 4, 1.0, rows)
        hi, lo = split(rows)
        for s in steps:
            ref[s, 272:288, lo_lane : lo_lane + n] = hi
            ref[s, 304:320, lo_lane : lo_lane + n] = lo
            ref[s, 336:352, lo_lane : lo_lane + n] = hi

    def forward(net, s, lanes, stencil, courant, ax, h2, s1, s2, st, cf):
        hi, lo = split(stencil)
        ax[s, 256:272, lanes] = hi
        ax[s, 288:304, lanes] = lo
        ax[s, 320:336, lanes] = hi
        st[s, :, lanes] = stencil
        one = dot(w1s[net, :, 0:96], ax[s, 256:352, lanes])
        yield
        one = jnp.tanh(one)
        s1[s, :, lanes] = 1.0 - one * one
        pair = stack(one)
        ax[s, 0:256, lanes] = pair
        yield
        out = dot(w2s[net], pair)
        yield
        bias = b2s[net]
        n = out.shape[1]
        bias = jnp.concatenate([bias] * (n // WIDTH), 1)
        two = jnp.tanh(out[0:128] + out[128:256] + bias)
        s2[s, :, lanes] = 1.0 - two * two
        pair = stack(two)
        h2[s, :, lanes] = pair
        yield
        out = dot(w3s[net], pair)
        yield
        coef = out[0:16] + out[16:32] + jnp.concatenate([b3s[net]] * (n // WIDTH), 1)
        cf[s, :, lanes] = coef
        terms = coef * stencil
        half = terms[0:8] + terms[8:16]
        return courant * (half + turn(half))

    def backward(net, s, lanes, dflux, courant, d1, d2, pb, s1, s2, st, cf, last=False):
        dq = courant * dflux
        dq = jnp.concatenate([dq, dq], 0)
        weighted = dq * st[s, :, lanes]
        hi, lo = split(weighted)
        pb[0:16, lanes] = hi
        pb[16:32, lanes] = lo
        yield
        two = dot(w3e[net, :, 0:48], jnp.concatenate([hi, lo, hi], 0))
        yield
        two = two * s2[s, :, lanes]
        pair = stack(two)
        d2[:, lanes] = pair
        yield
        out = dot(w2b[net], pair)
        yield
        one = (out[0:128] + out[128:256]) * s1[s, :, lanes]
        pair = stack(one)
        d1[:, lanes] = pair
        if last:
            return None, weighted
        yield
        out = dot(w1b[net], pair)
        yield
        return out[0:16] + out[16:32] + cf[s, :, lanes] * dq, weighted

    def quads(x, m, n):
        return (x[0:m, 0:n] + x[m : 2 * m, n : 2 * n]) + (x[0:m, n : 2 * n] + x[m : 2 * m, 0:n])

    def weight_grads(net, s, lanes, ax, h2, d1, d2, pb):
        out = dot_nt(ax[s, 0:288, lanes], d2[:, lanes])
        grads[net * NET_ROWS : net * NET_ROWS + 128] += quads(out, 128, 128)
        accb2[net] += out[256:288, 0:128] + out[256:288, 128:256]
        out = dot_nt(ax[s, 256:320, lanes], d1[:, lanes])
        grads[net * NET_ROWS + 128 : (net + 1) * NET_ROWS] += quads(out, 32, 128)
        out = dot_nt(pb[:, lanes], h2[s, :, lanes])
        acc3[net] += quads(out, 16, 128)

    def lane_fold(x):
        out = x[:, 0:128]
        for i in range(1, x.shape[1] // 128):
            out = out + x[:, 128 * i : 128 * (i + 1)]
        return out

    zchunks = (slice(0, 256), slice(256, 512), slice(512, 640))

    def zonal_stencil():
        c = line[...]
        return jnp.concatenate(
            [pick(lane_roll(c, 1), c), pick(lane_roll(c, -1), lane_roll(c, -2))], 0
        )

    def zonal(s):
        stencil = zonal_stencil()
        parts = run(
            [
                forward(
                    0, s, lanes, stencil[:, lanes], zcour[:, lanes], ax_z, h2_z, s1_z, s2_z, st_z, cf_z
                )
                for lanes in zchunks
            ]
        )
        flux = jnp.concatenate(parts, 1)
        new = line[...] - (flux - lane_roll(flux, 1))
        return pick(*from_line(new))

    def face_stencil(s, face):
        mid = turn(halo[s, 2])
        if face == 1:
            return jnp.concatenate([halo[s, 1], halo[s, 2]], 0)
        if face == -1:
            return jnp.concatenate([halo[s, 0], halo[s, 1]], 0)
        if face == 5:
            return jnp.concatenate([halo[s, 3], halo[s, 4]], 0)
        if face == 3:
            return jnp.concatenate([halo[s, 2], halo[s, 3]], 0)
        if face == 2:
            return jnp.concatenate([pick(turn(halo[s, 1]), mid), pick(mid, turn(halo[s, 3]))], 0)
        if face == 0:
            before = turn(halo[s, 1])
            return jnp.concatenate([pick(turn(halo[s, 0]), before), pick(before, mid)], 0)
        after = turn(halo[s, 3])
        return jnp.concatenate([pick(mid, after), pick(after, turn(halo[s, 4]))], 0)

    def merid_faces(s, slots):
        fluxes = []
        for slot in slots:
            lanes = slice(slot * NY, (slot + 1) * NY)
            fluxes.append(
                forward(
                    1,
                    s,
                    lanes,
                    face_stencil(s, SLOT_FACE[slot]),
                    mcour[:, lanes],
                    ax_m,
                    h2_m,
                    s1_m,
                    s2_m,
                    st_m,
                    cf_m,
                )
            )
        return run(fluxes)

    routes = ((1, 1), (-1, 3), (2, 0), (-2, 4))

    def inside(b):
        return (b >= 0) & (b < bands)

    def halo_copy(buf, s, which, send, recv):
        delta, slot = routes[which]
        return pltpu.make_async_remote_copy(
            src_ref=buf.at[s, 2],
            dst_ref=buf.at[s, slot],
            send_sem=send.at[which],
            recv_sem=recv.at[s, which],
            device_id=band_device(place(jnp.clip(mine + delta, 0, bands - 1))),
            device_id_type=LOGICAL,
        )

    def halo_start(buf, s, send, recv, which_all):
        for which in which_all:

            @pl.when(inside(mine + routes[which][0]))
            def _():
                halo_copy(buf, s, which, send, recv).start()

    def halo_wait(buf, s, send, recv, which_all):
        for which in which_all:

            @pl.when(inside(mine - routes[which][0]))
            def _():
                halo_copy(buf, s, which, send, recv).wait_recv()

    def halo_drain(buf, s, send, recv, which_all):
        for which in which_all:

            @pl.when(inside(mine + routes[which][0]))
            def _():
                halo_copy(buf, s, which, send, recv).wait_send()

    def move_copy(src, buf, which, send, recv):
        delta, slot = routes[which] if which < 4 else (0, 2)
        return pltpu.make_async_remote_copy(
            src_ref=src,
            dst_ref=buf.at[0, slot],
            send_sem=send.at[which],
            recv_sem=recv.at[0, which],
            device_id=band_device(place(jnp.clip(band + delta, 0, bands - 1))),
            device_id_type=LOGICAL,
        )

    def move_delta(which):
        return routes[which][0] if which < 4 else 0

    def move_start(src, buf, send, recv, which_all):
        for which in which_all:
            delta = move_delta(which)
            here = band + delta == mine

            @pl.when(inside(band + delta) & jnp.logical_not(here))
            def _():
                move_copy(src, buf, which, send, recv).start()

            @pl.when(here)
            def _():
                buf[0, routes[which][1] if which < 4 else 2] = src[...]

    def move_wait(src, buf, send, recv, which_all):
        for which in which_all:
            delta = move_delta(which)

            @pl.when(inside(mine - delta) & (mine - delta != band))
            def _():
                move_copy(src, buf, which, send, recv).wait_recv()

    def move_drain(src, buf, send, recv, which_all):
        for which in which_all:
            delta = move_delta(which)

            @pl.when(inside(band + delta) & (band + delta != mine))
            def _():
                move_copy(src, buf, which, send, recv).wait_send()

    def swap_copy(src, dst, index):
        return pltpu.make_async_remote_copy(
            src_ref=src,
            dst_ref=dst,
            send_sem=swap_send.at[index],
            recv_sem=swap_recv.at[index],
            device_id=band_device(mine),
            device_id_type=LOGICAL,
        )

    for copy in inputs:
        copy.wait()
    def block_of(ref):
        rows = [ref[b, 0, r : r + 1, :] for r in range(2) for b in range(4)]
        return jnp.concatenate(rows, 0)

    def zonal_constants(slab, steps):
        zw = to_line(slab[4:5, :], slab[5:6, :])
        zs = to_line(slab[2:3, :], slab[3:4, :])
        courant = 0.5 * (zw + lane_roll(zw, -1))
        zcour[...] = jnp.broadcast_to(courant, (8, NZ))
        constant_rows(ax_z, 0, courant, zs, lane_roll(zs, -1), steps)

    def merid_constants(slots, steps):
        def row(i, at):
            block, which = (i + 1) // 2, at + (i + 1) % 2
            return winds[0, block, which : which + 1, :]

        for slot in slots:
            face = SLOT_FACE[slot]
            courant = 0.5 * (row(face + 1, 0) + row(face + 2, 0))
            mcour[:, slot * NY : (slot + 1) * NY] = jnp.broadcast_to(courant, (8, NY))
            constant_rows(ax_m, slot * NY, courant, row(face + 1, 2), row(face + 2, 2), steps)

    with mark("prepare"):
        prepare(0)
        conc_out[...] = block_of(conc_ref)
        target_out[...] = block_of(target_ref)
        slab = jnp.concatenate(
            [mwind_ref[0], sea_ref[...].astype(F32), zwind_ref[0], zwind_ref[0]], 0
        )
        wind_out[...] = slab
        line[...] = to_line(*both_rows(conc_out[...]))
        zonal_constants(slab, range(STEPS))
        for acc in (grads, acc3, accb2, accp):
            acc[...] = jnp.zeros_like(acc)
    with mark("zonal"):
        block_out[...] = zonal(0)
    with mark("barrier"):
        pl.semaphore_wait(barrier, greeted)
    move_start(block_out, halo, halo_send, halo_recv, (0, 1, 4))
    move_start(wind_out, winds, wind_send, wind_recv, (0, 1, 4))
    move_start(block_out, halo, halo_send, halo_recv, (2, 3))
    move_start(wind_out, winds, wind_send, wind_recv, (2, 3))
    move_start(target_out, targets, target_send, target_recv, (0, 1, 4))

    @pl.when(moved)
    def _():
        swap_copy(conc_out, conc_in, 0).start()

    @pl.when(jnp.logical_not(moved))
    def _():
        conc_in[...] = conc_out[...]

    with mark("prepare1"):
        prepare(1)
    with mark("waitwind"):
        move_wait(wind_out, winds, wind_send, wind_recv, (0, 1, 4))
    with mark("constants"):
        merid_constants((0, 1, 2, 3, 4), range(STEPS))

        @pl.when(moved)
        def _():
            zonal_constants(winds[0, 2], range(STEPS))

    with mark("waitmove"):
        move_wait(block_out, halo, halo_send, halo_recv, (0, 1, 4))

    def merid(s):
        with mark("merid"):
            f1, f2, f3 = merid_faces(s, (0, 1, 2))
            new = halo[s, 2] - pick(f2 - f1, f3 - f2)
            line[...] = to_line(*both_rows(new))
        return new

    move_drain(block_out, halo, halo_send, halo_recv, (0, 1, 2, 3, 4))
    merid(0)

    def halo_step(s):
        with mark("zonal"):
            halo[s, 2] = zonal(s)
        halo_start(halo, s, halo_send, halo_recv, (0, 1, 2, 3))

    halo_step(1)
    with mark("redundant"):
        move_wait(block_out, halo, halo_send, halo_recv, (2, 3))
        merid_faces(0, (3, 4))
        move_wait(wind_out, winds, wind_send, wind_recv, (2, 3))
        merid_constants((5, 6), (STEPS - 1,))

    with mark("waithalo"):
        halo_wait(halo, 1, halo_send, halo_recv, (0, 1))
    halo_drain(halo, 1, halo_send, halo_recv, (0, 1, 2, 3))
    merid(1)
    halo_step(2)
    with mark("redundant"):
        halo_wait(halo, 1, halo_send, halo_recv, (2, 3))
        merid_faces(1, (3, 4))

    @pl.when(moved)
    def _():
        with mark("zonal_again"):
            swap_copy(conc_out, conc_in, 0).wait_recv()
            line[...] = to_line(*both_rows(conc_in[...]))
            zonal(0)

    move_wait(target_out, targets, target_send, target_recv, (0, 1, 4))
    with mark("waithalo"):
        halo_wait(halo, 2, halo_send, halo_recv, (0, 1))
    halo_drain(halo, 2, halo_send, halo_recv, (0, 1, 2, 3))
    with mark("merid"):
        f1, f2, f3 = merid_faces(2, (0, 1, 2))
    with mark("waittwo"):
        halo_wait(halo, 2, halo_send, halo_recv, (2, 3))
    with mark("merid4"):
        f0, f4, f9, f5 = merid_faces(2, (3, 4, 5, 6))
    new = halo[2, 2] - pick(f2 - f1, f3 - f2)
    before = halo[2, 1] - pick(f0 - f9, f1 - f0)
    after = halo[2, 3] - pick(f4 - f3, f5 - f4)
    ghalo[2, 2] = (new - targets[0, 2]) * loss_scale
    ghalo[2, 1] = jnp.where(mine > 0, (before - targets[0, 1]) * loss_scale, 0.0)
    ghalo[2, 3] = jnp.where(mine < bands - 1, (after - targets[0, 3]) * loss_scale, 0.0)
    final_out[...] = new

    @pl.when(moved)
    def _():
        swap_copy(final_out, final_in, 1).start()

    def merid_back(s):
        @pl.when(s < STEPS - 1)
        def _():
            with mark("waitg"):
                halo_wait(ghalo, s, ghalo_send, ghalo_recv, (0, 1))
            halo_drain(ghalo, s, ghalo_send, ghalo_recv, (0, 1))

        g = []
        for block in (1, 2, 3):
            g.extend(both_rows(ghalo[s, block]))
        lows, highs = [None] * 5, [None] * 5
        first = None
        inner = None
        parts = []
        for slot, face in enumerate(SLOT_FACE[:5]):
            lanes = slice(slot * NY, (slot + 1) * NY)
            part = backward(
                1,
                s,
                lanes,
                g[face + 1] - g[face],
                mcour[:, lanes],
                d1_m,
                d2_m,
                pb_m,
                s1_m,
                s2_m,
                st_m,
                cf_m,
            )
            parts.append(part)
        for slot, (out, weighted) in enumerate(run(parts)):
            face = SLOT_FACE[slot]
            lows[face], highs[face] = out[0:8], out[8:16]
            if slot == 0:
                first = lane_fold(weighted)
            elif slot == 1:
                inner = lane_fold(weighted)
            elif slot == 2:
                inner = inner + lane_fold(weighted)
        new = ghalo[s, 2] + (highs[1] + lows[3])
        new = new + turn(pick(highs[2] + lows[4], highs[0] + lows[2]))
        accp[1] += inner

        @pl.when(mine == 0)
        def _():
            accp[1] += first

        gline[...] = to_line(*both_rows(new))

    def zonal_back(s, last=False):
        gz = gline[...]
        dflux = lane_roll(gz, -1) - gz
        outs = run(
            [
                backward(
                    0,
                    s,
                    lanes,
                    dflux[:, lanes],
                    zcour[:, lanes],
                    d1_z,
                    d2_z,
                    pb_z,
                    s1_z,
                    s2_z,
                    st_z,
                    cf_z,
                    last,
                )
                for lanes in zchunks
            ]
        )
        accp[0] += sum(lane_fold(o[1]) for o in outs)
        if last:
            return None
        out = jnp.concatenate([o[0] for o in outs], 1)
        low, high = out[0:8], out[8:16]
        t = pick(lane_roll(low, -1), low) + pick(lane_roll(high, 1), lane_roll(high, 2))
        new = gz + t + turn(t)

        return pick(*from_line(new))

    def merid_weights(s):
        weight_grads(1, s, slice(NY, 3 * NY), ax_m, h2_m, d1_m, d2_m, pb_m)

        @pl.when(mine == 0)
        def _():
            weight_grads(1, s, slice(0, NY), ax_m, h2_m, d1_m, d2_m, pb_m)

    def zonal_weights(s):
        weight_grads(0, s, slice(0, NZ), ax_z, h2_z, d1_z, d2_z, pb_z)

    def backward_step(i, carry):
        s = STEPS - 1 - i
        merid_back(s)
        ghalo[s - 1, 2] = zonal_back(s)
        halo_start(ghalo, s - 1, ghalo_send, ghalo_recv, (0, 1))
        with mark("weights"):
            merid_weights(s)
            zonal_weights(s)
        return carry

    lax.fori_loop(0, STEPS - 1, backward_step, 0)

    centre = jnp.where(
        lax.broadcasted_iota(jnp.int32, (16, 16), 1) // 4
        == lax.broadcasted_iota(jnp.int32, (16, 16), 0),
        0.75,
        -0.25,
    )
    centre = jnp.concatenate([centre, centre], 1).astype(BF16)

    def gather_net(net):
        top = net * NET_ROWS
        grads[top + 149 : top + 150] = accb2[net, 20:21, :]
        grads[top + 152 : top + 156] = dot(centre, stack(acc3[net]))[0:4]
        sums = jnp.sum(accp[net], 1, keepdims=True)
        mine = (
            lax.broadcasted_iota(jnp.int32, (16, WIDTH), 0) // 4
            == lax.broadcasted_iota(jnp.int32, (16, WIDTH), 1)
        )
        row = jnp.sum(jnp.where(mine, sums, 0.0), 0, keepdims=True)
        grads[top + 156 : top + 157] = row - jnp.sum(row, 1, keepdims=True) * 0.25

    piece = GRAD_ROWS // levs
    part = piece // side_y
    started = []

    def send(src, dst, phase, device):
        pltpu.make_async_remote_copy(
            src_ref=src,
            dst_ref=dst,
            send_sem=red_send.at[phase],
            recv_sem=red_recv.at[phase],
            device_id=device,
            device_id_type=LOGICAL,
        ).start()

    def wait(buf, count, phase):
        with mark("wait_ar"):
            some = buf.at[0:count]
            pltpu.make_async_copy(some, some, red_recv.at[phase]).wait()
        started.append((some, phase))

    wide = levs // 2
    my_x = lax.div(lev, 2)
    core = lev - 2 * my_x

    def first_copy(net, k):
        tx = wrap(my_x + k, wide)
        slot = 2 * k + core
        row = pl.multiple_of(net * NET_ROWS + tx * piece, 8)
        return pltpu.make_async_remote_copy(
            src_ref=grads.at[pl.ds(row, piece)],
            dst_ref=r1.at[slot],
            send_sem=red_send.at[0],
            recv_sem=red_recv.at[0],
            device_id=lev_device(2 * tx + net),
            device_id_type=LOGICAL,
        )

    def send_net(net):
        for k in far_first(wide):
            first_copy(net, k).start()

        @pl.when(core != net)
        def _():
            first_copy(net, 0).start()

    merid_back(0)
    with mark("wg1"):
        merid_weights(0)
    with mark("gather1"):
        gather_net(1)
        send_net(1)
    with mark("zback0"):
        zonal_back(0, True)
    with mark("wg0"):
        zonal_weights(0)
    with mark("gather0"):
        gather_net(0)
        send_net(0)
    @pl.when(moved)
    def _():
        swap_copy(final_out, final_in, 1).wait()
        swap_copy(conc_out, conc_in, 0).wait_send()

    final = jnp.where(moved, final_in[...], final_out[...])
    for r in range(2):
        for b in range(4):
            field_ref[b, 0, r : r + 1, :] = final[4 * r + b : 4 * r + b + 1, :]
    move_drain(wind_out, winds, wind_send, wind_recv, (0, 1, 2, 3, 4))
    move_drain(target_out, targets, target_send, target_recv, (0, 1, 4))

    row = pl.multiple_of(core * NET_ROWS + my_x * piece, 8)
    with mark("wait_ar"):
        wait(r1, levs - 1, 0)
        total = grads[pl.ds(row, piece)] + r1[1 - core]
        for k in range(1, wide):
            for c in range(2):
                total = total + r1[2 * k + c]
    for i in range(side_y):
        s1buf[i] = total[i * part : (i + 1) * part]
    for d in far_first(side_y):
        ty = wrap(my_y + d, side_y)
        send(s1buf.at[ty], r2.at[d - 1], 1, y_device(ty))
    total = s1buf[my_y]
    wait(r2, side_y - 1, 1)
    for d in range(1, side_y):
        total = total + r2[d - 1]
    r3[my_z] = total
    for d in far_first(side_z):
        tz = wrap(my_z + d, side_z)
        send(r3.at[my_z], r3.at[my_z], 2, z_device(tz))
    wait(r3, side_z - 1, 2)
    total = r3[0]
    for i in range(1, side_z):
        total = total + r3[i]
    a4[my_y] = total
    for d in far_first(side_y):
        ty = wrap(my_y + d, side_y)
        send(a4.at[my_y], a4.at[my_y], 3, y_device(ty))
    wait(a4, side_y - 1, 3)
    for i in range(side_y):
        full[lev, i * part : (i + 1) * part] = a4[i]
    for d in sorted(range(1, levs), key=lambda d: -min(d // 2, wide - d // 2)):
        tl = wrap(lev + d, levs)
        send(full.at[lev], full.at[lev], 4, lev_device(tl))
    wait(full, levs - 1, 4)
    for net in range(2):
        everything = jnp.concatenate([full[2 * x + net] for x in range(wide)], 0)
        top = 0
        gw2_ref[net] = everything[top : top + 128]
        gw1_ref[:, net, :] = everything[top + 128 : top + 148]
        gb1_ref[net : net + 1] = everything[top + 148 : top + 149]
        gb2_ref[net : net + 1] = everything[top + 149 : top + 150]
        gw3_ref[net] = everything[top + 152 : top + 156]
        gb3_ref[net : net + 1] = everything[top + 156 : top + 157, 0:4]

    for some, phase in started:
        pltpu.make_async_copy(some, some, red_send.at[phase]).wait()


def on_device(bands, levs, loss_scale, *args):
    piece = GRAD_ROWS // levs
    side_y = math.isqrt(bands)
    side_z = bands // side_y
    part = piece // side_y
    vmem = pltpu.VMEM
    sweeps = [NZ, NM]
    back = [NZ, NB]
    args = list(args)
    args[5] = jnp.transpose(args[5], (1, 0, 2))
    scratch = [
        *[vmem(arg.shape, arg.dtype) for arg in args],
        pltpu.SemaphoreType.DMA((len(args),)),
        vmem((2, 128, 128), BF16),
        vmem((2, 256, 256), BF16),
        vmem((2, 32, 256), BF16),
        vmem((2, 128, 128), BF16),
        vmem((2, 256, 256), BF16),
        vmem((2, 32, 256), BF16),
        vmem((2, 128, 128), F32),
        vmem((2, 16, 128), F32),
        vmem((8, NZ), F32),
        vmem((8, NM), F32),
        vmem((STEPS, 5, 8, NY), F32),
        vmem((STEPS, 5, 8, NY), F32),
        vmem((1, 5, 8, NY), F32),
        vmem((8, NY), F32),
        vmem((8, NY), F32),
        vmem((8, NY), F32),
        vmem((8, NY), F32),
        vmem((8, NY), F32),
        vmem((1, 5, 8, NY), F32),
        vmem((8, NY), F32),
        vmem((8, NY), F32),
        vmem((8, NZ), F32),
        vmem((8, NZ), F32),
        *[vmem((STEPS, 352, n), BF16) for n in sweeps],
        *[vmem((STEPS, 256, n), BF16) for n in sweeps],
        *[vmem((STEPS, 128, n), F32) for n in sweeps],
        *[vmem((STEPS, 128, n), F32) for n in sweeps],
        *[vmem((STEPS, 16, n), F32) for n in sweeps],
        *[vmem((STEPS, 16, n), F32) for n in sweeps],
        *[vmem((256, n), BF16) for n in back],
        *[vmem((256, n), BF16) for n in back],
        *[vmem((32, n), BF16) for n in back],
        vmem((2, 16, 128), F32),
        vmem((2, 32, 128), F32),
        vmem((2, 16, 128), F32),
        vmem((GRAD_ROWS, 128), F32),
        vmem((levs, piece, 128), F32),
        vmem((side_y, part, 128), F32),
        vmem((side_y - 1, part, 128), F32),
        vmem((side_z, part, 128), F32),
        vmem((side_y, part, 128), F32),
        vmem((levs, piece, 128), F32),
        pltpu.SemaphoreType.DMA((5,)),
        pltpu.SemaphoreType.DMA((STEPS, 5)),
        pltpu.SemaphoreType.DMA((2,)),
        pltpu.SemaphoreType.DMA((STEPS, 2)),
        pltpu.SemaphoreType.DMA((5,)),
        pltpu.SemaphoreType.DMA((1, 5)),
        pltpu.SemaphoreType.DMA((5,)),
        pltpu.SemaphoreType.DMA((1, 5)),
        pltpu.SemaphoreType.DMA((2,)),
        pltpu.SemaphoreType.DMA((2,)),
        pltpu.SemaphoreType.DMA((5,)),
        pltpu.SemaphoreType.DMA((5,)),
    ]
    out_shape = [jax.ShapeDtypeStruct(args[0].shape, F32)] + [
        jax.ShapeDtypeStruct(args[i].shape, F32) for i in range(5, 11)
    ]
    results = pl.pallas_call(
        functools.partial(kernel, bands, levs, loss_scale),
        out_shape=out_shape,
        in_specs=[pl.BlockSpec(memory_space=pltpu.HBM)] * 11,
        out_specs=[pl.BlockSpec(memory_space=pltpu.VMEM)] * 7,
        scratch_shapes=scratch,
        compiler_params=pltpu.CompilerParams(
            collective_id=0, has_side_effects=True, vmem_limit_bytes=48 * 1024 * 1024
        ),
        name="advection_step",
    )(*[pltpu.with_memory_space_constraint(arg, pltpu.HBM) for arg in args])
    results = list(
        pl.pallas_call(
            write_out,
            out_shape=out_shape,
            in_specs=[pl.BlockSpec(memory_space=pltpu.VMEM)] * 7,
            out_specs=[pl.BlockSpec(memory_space=pltpu.HBM)] * 7,
            scratch_shapes=[pltpu.SemaphoreType.DMA((7,))],
            compiler_params=pltpu.CompilerParams(vmem_limit_bytes=1024 * 1024),
            name="write_out",
        )(*results)
    )
    results[1] = jnp.transpose(results[1], (1, 0, 2))
    return tuple(results)


def write_out(*refs):
    sem = refs[14]
    copies = [pltpu.make_async_copy(refs[i], refs[7 + i], sem.at[i]) for i in range(7)]
    for copy in copies:
        copy.start()
    for copy in copies:
        copy.wait()


def solution(mesh):
    bands, levs = mesh.shape["band"], mesh.shape["lev"]
    loss_scale = 1.0 / math.sqrt(4 * levs * 2 * bands * NY)
    return jax.shard_map(
        functools.partial(on_device, bands, levs, loss_scale),
        mesh=mesh,
        in_specs=(
            P(None, "lev", "band", None),
            P(None, "lev", "band", None),
            P("lev", "band", None),
            P("lev", "band", None),
            P("band", None),
            P(),
            P(),
            P(),
            P(),
            P(),
            P(),
        ),
        out_specs=(P(None, "lev", "band", None), P(), P(), P(), P(), P(), P()),
        check_vma=False,
    )
```

```python
import contextlib
import functools
import math

import jax
import jax.numpy as jnp
from jax import lax
from jax.experimental import pallas as pl
from jax.experimental.pallas import tpu as pltpu
from jax.sharding import PartitionSpec as P

STEPS = 3
WIDTH = 128
F32 = jnp.float32
BF16 = jnp.bfloat16
LOGICAL = pl.DeviceIdType.LOGICAL
BASE = (-1.0 / 12.0, 7.0 / 12.0, 7.0 / 12.0, -1.0 / 12.0)

NY = 256
GAP = 64
NZ = 640
SLOT_FACE = (1, 2, 3, 0, 4, -1, 5)
NM = 7 * NY
NB = 5 * NY
NET_ROWS = 160
GRAD_ROWS = 2 * NET_ROWS


def mark(name):
    return contextlib.nullcontext()


def split(x):
    hi = x.astype(BF16)
    lo = (x - hi.astype(F32)).astype(BF16)
    return hi, lo


def stack(x):
    return jnp.concatenate(split(x), axis=0)


def dot(a, b):
    return lax.dot_general(a, b, (((1,), (0,)), ((), ())), preferred_element_type=F32)


def dot_nt(a, b):
    return lax.dot_general(a, b, (((1,), (1,)), ((), ())), preferred_element_type=F32)


def run(parts, skew=0):
    results = [None] * len(parts)
    live = set(range(len(parts)))
    tick = 0
    while live:
        for i in sorted(live):
            if tick >= i * skew:
                try:
                    next(parts[i])
                except StopIteration as stop:
                    results[i] = stop.value
                    live.discard(i)
        tick += 1
    return results


def far_first(n):
    return sorted(range(1, n), key=lambda d: -min(d, n - d))


def low_half(shape):
    return lax.broadcasted_iota(jnp.int32, shape, 0) < 4


def pick(a, b):
    return jnp.where(low_half(a.shape), a, b)


def turn(x):
    return pltpu.roll(x, 4, axis=0)


def lane_roll(x, shift):
    return pltpu.roll(x, shift % x.shape[1], axis=1)


def both_rows(block):
    turned = turn(block)
    return pick(block, turned), pick(turned, block)


def to_line(first, second):
    gap = jnp.zeros((first.shape[0], 2 * GAP), F32)
    return jnp.concatenate([lane_roll(jnp.concatenate([first, gap], 1), GAP), second], 1)


def from_line(line):
    return lane_roll(line[:, : NY + 2 * GAP], -GAP)[:, :NY], line[:, NY + 2 * GAP :]


def kernel(
    bands,
    levs,
    loss_scale,
    conc_hbm,
    target_hbm,
    zwind_hbm,
    mwind_hbm,
    sea_hbm,
    w1_hbm,
    b1_hbm,
    w2_hbm,
    b2_hbm,
    w3_hbm,
    b3_hbm,
    field_ref,
    gw1_ref,
    gb1_ref,
    gw2_ref,
    gb2_ref,
    gw3_ref,
    gb3_ref,
    conc_ref,
    target_ref,
    zwind_ref,
    mwind_ref,
    sea_ref,
    w1_ref,
    b1_ref,
    w2_ref,
    b2_ref,
    w3_ref,
    b3_ref,
    input_sem,
    w1s,
    w2s,
    w3s,
    w3e,
    w2b,
    w1b,
    b2s,
    b3s,
    zcour,
    mcour,
    halo,
    ghalo,
    winds,
    block_out,
    wind_out,
    conc_out,
    conc_in,
    target_out,
    targets,
    final_out,
    final_in,
    line,
    gline,
    ax_z,
    ax_m,
    h2_z,
    h2_m,
    s1_z,
    s1_m,
    s2_z,
    s2_m,
    st_z,
    st_m,
    cf_z,
    cf_m,
    d1_z,
    d1_m,
    d2_z,
    d2_m,
    pb_z,
    pb_m,
    acc3,
    accb2,
    accp,
    grads,
    r1,
    s1buf,
    r2,
    r3,
    a4,
    full,
    halo_send,
    halo_recv,
    ghalo_send,
    ghalo_recv,
    wind_send,
    wind_recv,
    target_send,
    target_recv,
    swap_send,
    swap_recv,
    red_send,
    red_recv,
):
    side_y = math.isqrt(bands)
    side_z = bands // side_y
    band = lax.axis_index("band")
    lev = lax.axis_index("lev")
    my_y = lax.div(band, side_z)
    my_z = lax.rem(band, side_z)

    def place(b):
        y = lax.div(b, side_z)
        z = b - y * side_z
        return b + lax.rem(y, 2) * (side_z - 1 - 2 * z)

    mine = place(band)
    moved = mine != band

    def wrap(at, n):
        return jnp.where(at >= n, at - n, at)

    def y_device(ty):
        return (ty * side_z + my_z) * levs + lev

    def z_device(tz):
        return (my_y * side_z + tz) * levs + lev

    def lev_device(tl):
        return band * levs + tl

    def band_device(tb):
        return tb * levs + lev

    inputs = [
        pltpu.make_async_copy(src, dst, input_sem.at[i])
        for i, (src, dst) in enumerate(
            (
                (w2_hbm, w2_ref),
                (w1_hbm, w1_ref),
                (b1_hbm, b1_ref),
                (b2_hbm, b2_ref),
                (w3_hbm, w3_ref),
                (b3_hbm, b3_ref),
                (conc_hbm, conc_ref),
                (zwind_hbm, zwind_ref),
                (sea_hbm, sea_ref),
                (mwind_hbm, mwind_ref),
                (target_hbm, target_ref),
            )
        )
    ]
    for copy in inputs:
        copy.start()

    winds[...] = jnp.zeros_like(winds)
    halo[...] = jnp.zeros_like(halo)
    ghalo[...] = jnp.zeros_like(ghalo)
    targets[...] = jnp.zeros_like(targets)
    barrier = pltpu.get_barrier_semaphore()
    greeted = 0
    for d in range(1, levs):
        pl.semaphore_signal(
            barrier, inc=1, device_id=lev_device(wrap(lev + d, levs)), device_id_type=LOGICAL
        )
        greeted += 1
    for d in range(1, side_y):
        pl.semaphore_signal(
            barrier, inc=1, device_id=y_device(wrap(my_y + d, side_y)), device_id_type=LOGICAL
        )
        greeted += 1
    for d in range(1, side_z):
        pl.semaphore_signal(
            barrier, inc=1, device_id=z_device(wrap(my_z + d, side_z)), device_id_type=LOGICAL
        )
        greeted += 1

    near_end = (my_z < 2) | (my_z >= side_z - 2)

    def others():
        for delta in (1, -1, 2, -2):
            for base, mapped in ((band, True), (mine, False), (mine, True)):
                at = base + delta
                known = (at >= 0) & (at < bands)
                at = jnp.clip(at, 0, bands - 1)
                device = place(at) if mapped else at
                yield device, near_end & known & (lax.div(device, side_z) != my_y)

    @pl.when(near_end)
    def _():
        for device, other in others():

            @pl.when(other)
            def _():
                pl.semaphore_signal(
                    barrier, inc=1, device_id=band_device(device), device_id_type=LOGICAL
                )

    for _, other in others():
        greeted = greeted + other.astype(jnp.int32)

    def prepare(net):
        w1 = w1_ref[:, net, :]
        b1 = b1_ref[net : net + 1, :]
        rows = jnp.concatenate([w1, b1, jnp.zeros((11, WIDTH), F32)], 0)
        hi, lo = split(rows)
        hi, lo = hi.astype(F32), lo.astype(F32)
        w1s[net] = jnp.concatenate([hi, hi, lo, jnp.zeros_like(hi)], 0).T.astype(BF16)
        hi, lo = split(rows[0:16])
        w1b[net, 0:16, 0:128] = hi
        w1b[net, 0:16, 128:256] = hi
        w1b[net, 16:32, 0:128] = lo
        w1b[net, 16:32, 128:256] = lo
        w2 = w2_ref[net]
        for ref, mat in ((w2s, w2.T), (w2b, w2)):
            hi, lo = split(mat)
            ref[net, 0:128, 0:128] = hi
            ref[net, 0:128, 128:256] = hi
            ref[net, 128:256, 0:128] = lo
            ref[net, 128:256, 128:256] = lo
        b2s[net] = jnp.broadcast_to(b2_ref[net : net + 1, :], (WIDTH, WIDTH)).T
        w3 = w3_ref[net]
        w3 = w3 - jnp.mean(w3, 0, keepdims=True)
        group = lax.broadcasted_iota(jnp.int32, (16, WIDTH), 0) // 4
        rep = jnp.zeros((16, WIDTH), F32)
        for j in range(4):
            rep = jnp.where(group == j, w3[j : j + 1, :], rep)
        hi, lo = split(rep)
        w3s[net, 0:16, 0:128] = hi
        w3s[net, 0:16, 128:256] = hi
        w3s[net, 16:32, 0:128] = lo
        w3s[net, 16:32, 128:256] = lo
        hi, lo = hi.astype(F32), lo.astype(F32)
        w3e[net] = jnp.concatenate([hi, hi, lo, jnp.zeros((80, WIDTH), F32)], 0).T.astype(BF16)
        b3 = b3_ref[net : net + 1, :]
        b3 = b3 - jnp.mean(b3, 1, keepdims=True)
        mine = (
            lax.broadcasted_iota(jnp.int32, (16, 4), 0) // 4
            == lax.broadcasted_iota(jnp.int32, (16, 4), 1)
        )
        column = jnp.sum(jnp.where(mine, b3, 0.0), 1, keepdims=True)
        place = lax.broadcasted_iota(jnp.int32, (16, WIDTH), 0) // 4
        base = jnp.where((place == 0) | (place == 3), BASE[0], BASE[1])
        b3s[net] = column + base

    def constant_rows(ref, lo_lane, courant, low, high, steps):
        n = courant.shape[1]
        place = lax.broadcasted_iota(jnp.int32, (16, n), 0)
        rows = jnp.where(place == 0, courant, 0.0)
        rows = jnp.where(place == 1, courant * courant, rows)
        rows = jnp.where(place == 2, low, rows)
        rows = jnp.where(place == 3, high, rows)
        rows = jnp.where(place == 4, 1.0, rows)
        hi, lo = split(rows)
        for s in steps:
            ref[s, 272:288, lo_lane : lo_lane + n] = hi
            ref[s, 304:320, lo_lane : lo_lane + n] = lo
            ref[s, 336:352, lo_lane : lo_lane + n] = hi

    def forward(net, s, lanes, stencil, courant, ax, h2, s1, s2, st, cf):
        hi, lo = split(stencil)
        ax[s, 256:272, lanes] = hi
        ax[s, 288:304, lanes] = lo
        ax[s, 320:336, lanes] = hi
        st[s, :, lanes] = stencil
        one = dot(w1s[net, :, 0:96], ax[s, 256:352, lanes])
        yield
        one = jnp.tanh(one)
        s1[s, :, lanes] = 1.0 - one * one
        pair = stack(one)
        ax[s, 0:256, lanes] = pair
        yield
        out = dot(w2s[net], pair)
        yield
        bias = b2s[net]
        n = out.shape[1]
        bias = jnp.concatenate([bias] * (n // WIDTH), 1)
        two = jnp.tanh(out[0:128] + out[128:256] + bias)
        s2[s, :, lanes] = 1.0 - two * two
        pair = stack(two)
        h2[s, :, lanes] = pair
        yield
        out = dot(w3s[net], pair)
        yield
        coef = out[0:16] + out[16:32] + jnp.concatenate([b3s[net]] * (n // WIDTH), 1)
        cf[s, :, lanes] = coef
        terms = coef * stencil
        half = terms[0:8] + terms[8:16]
        return courant * (half + turn(half))

    def backward(net, s, lanes, dflux, courant, d1, d2, pb, s1, s2, st, cf, last=False):
        dq = courant * dflux
        dq = jnp.concatenate([dq, dq], 0)
        weighted = dq * st[s, :, lanes]
        hi, lo = split(weighted)
        pb[0:16, lanes] = hi
        pb[16:32, lanes] = lo
        yield
        two = dot(w3e[net, :, 0:48], jnp.concatenate([hi, lo, hi], 0))
        yield
        two = two * s2[s, :, lanes]
        pair = stack(two)
        d2[:, lanes] = pair
        yield
        out = dot(w2b[net], pair)
        yield
        one = (out[0:128] + out[128:256]) * s1[s, :, lanes]
        pair = stack(one)
        d1[:, lanes] = pair
        if last:
            return None, weighted
        yield
        out = dot(w1b[net], pair)
        yield
        return out[0:16] + out[16:32] + cf[s, :, lanes] * dq, weighted

    def quads(x, m, n):
        return (x[0:m, 0:n] + x[m : 2 * m, n : 2 * n]) + (x[0:m, n : 2 * n] + x[m : 2 * m, 0:n])

    def weight_stages(net, s, lanes, ax, h2, d1, d2, pb):
        out = dot_nt(ax[s, 0:288, lanes], d2[:, lanes])
        yield
        grads[net * NET_ROWS : net * NET_ROWS + 128] += quads(out, 128, 128)
        accb2[net] += out[256:288, 0:128] + out[256:288, 128:256]
        yield
        out = dot_nt(ax[s, 256:320, lanes], d1[:, lanes])
        yield
        grads[net * NET_ROWS + 128 : (net + 1) * NET_ROWS] += quads(out, 32, 128)
        out = dot_nt(pb[:, lanes], h2[s, :, lanes])
        yield
        acc3[net] += quads(out, 16, 128)

    def weight_grads(*args):
        run([weight_stages(*args)])

    def lane_fold(x):
        out = x[:, 0:128]
        for i in range(1, x.shape[1] // 128):
            out = out + x[:, 128 * i : 128 * (i + 1)]
        return out

    zchunks = (slice(0, 256), slice(256, 512), slice(512, 640))

    def zonal_many(parts):
        stages = []
        for at, which, c in parts:
            stencil = jnp.concatenate(
                [pick(lane_roll(c, 1), c), pick(lane_roll(c, -1), lane_roll(c, -2))], 0
            )
            for lanes in zchunks:
                stages.append(
                    forward(
                        0,
                        at,
                        lanes,
                        stencil[:, lanes],
                        zcour[which, :, lanes],
                        ax_z,
                        h2_z,
                        s1_z,
                        s2_z,
                        st_z,
                        cf_z,
                    )
                )
        fluxes = run(stages)
        blocks = []
        for i, (_, _, c) in enumerate(parts):
            flux = jnp.concatenate(fluxes[3 * i : 3 * i + 3], 1)
            blocks.append(pick(*from_line(c - (flux - lane_roll(flux, 1)))))
        return blocks

    def zonal(s):
        return zonal_many([(s, 0, line[...])])[0]

    def face_stencil(s, face):
        mid = turn(halo[s, 2])
        if face == 1:
            return jnp.concatenate([halo[s, 1], halo[s, 2]], 0)
        if face == -1:
            return jnp.concatenate([halo[s, 0], halo[s, 1]], 0)
        if face == 5:
            return jnp.concatenate([halo[s, 3], halo[s, 4]], 0)
        if face == 3:
            return jnp.concatenate([halo[s, 2], halo[s, 3]], 0)
        if face == 2:
            return jnp.concatenate([pick(turn(halo[s, 1]), mid), pick(mid, turn(halo[s, 3]))], 0)
        if face == 0:
            before = turn(halo[s, 1])
            return jnp.concatenate([pick(turn(halo[s, 0]), before), pick(before, mid)], 0)
        after = turn(halo[s, 3])
        return jnp.concatenate([pick(mid, after), pick(after, turn(halo[s, 4]))], 0)

    def merid_faces(s, slots):
        fluxes = []
        for slot in slots:
            lanes = slice(slot * NY, (slot + 1) * NY)
            fluxes.append(
                forward(
                    1,
                    s,
                    lanes,
                    face_stencil(s, SLOT_FACE[slot]),
                    mcour[:, lanes],
                    ax_m,
                    h2_m,
                    s1_m,
                    s2_m,
                    st_m,
                    cf_m,
                )
            )
        return run(fluxes)

    routes = ((1, 1), (-1, 3), (2, 0), (-2, 4))

    def inside(b):
        return (b >= 0) & (b < bands)

    def halo_copy(buf, s, which, send, recv):
        delta, slot = routes[which]
        return pltpu.make_async_remote_copy(
            src_ref=buf.at[s, 2],
            dst_ref=buf.at[s, slot],
            send_sem=send.at[which],
            recv_sem=recv.at[s, which],
            device_id=band_device(place(jnp.clip(mine + delta, 0, bands - 1))),
            device_id_type=LOGICAL,
        )

    def halo_start(buf, s, send, recv, which_all):
        for which in which_all:

            @pl.when(inside(mine + routes[which][0]))
            def _():
                halo_copy(buf, s, which, send, recv).start()

    def halo_wait(buf, s, send, recv, which_all):
        for which in which_all:

            @pl.when(inside(mine - routes[which][0]))
            def _():
                halo_copy(buf, s, which, send, recv).wait_recv()

    def halo_drain(buf, s, send, recv, which_all):
        for which in which_all:

            @pl.when(inside(mine + routes[which][0]))
            def _():
                halo_copy(buf, s, which, send, recv).wait_send()

    def move_copy(src, buf, which, send, recv):
        delta, slot = routes[which] if which < 4 else (0, 2)
        return pltpu.make_async_remote_copy(
            src_ref=src,
            dst_ref=buf.at[0, slot],
            send_sem=send.at[which],
            recv_sem=recv.at[0, which],
            device_id=band_device(place(jnp.clip(band + delta, 0, bands - 1))),
            device_id_type=LOGICAL,
        )

    def move_delta(which):
        return routes[which][0] if which < 4 else 0

    def move_start(src, buf, send, recv, which_all):
        for which in which_all:
            delta = move_delta(which)
            here = band + delta == mine

            @pl.when(inside(band + delta) & jnp.logical_not(here))
            def _():
                move_copy(src, buf, which, send, recv).start()

            @pl.when(here)
            def _():
                buf[0, routes[which][1] if which < 4 else 2] = src[...]

    def move_wait(src, buf, send, recv, which_all):
        for which in which_all:
            delta = move_delta(which)

            @pl.when(inside(mine - delta) & (mine - delta != band))
            def _():
                move_copy(src, buf, which, send, recv).wait_recv()

    def move_drain(src, buf, send, recv, which_all):
        for which in which_all:
            delta = move_delta(which)

            @pl.when(inside(band + delta) & (band + delta != mine))
            def _():
                move_copy(src, buf, which, send, recv).wait_send()

    def swap_copy(src, dst, index):
        return pltpu.make_async_remote_copy(
            src_ref=src,
            dst_ref=dst,
            send_sem=swap_send.at[index],
            recv_sem=swap_recv.at[index],
            device_id=band_device(mine),
            device_id_type=LOGICAL,
        )

    for copy in inputs:
        copy.wait()
    def block_of(ref):
        rows = [ref[b, 0, r : r + 1, :] for r in range(2) for b in range(4)]
        return jnp.concatenate(rows, 0)

    def zonal_constants(slab, steps, which=0):
        zw = to_line(slab[4:5, :], slab[5:6, :])
        zs = to_line(slab[2:3, :], slab[3:4, :])
        courant = 0.5 * (zw + lane_roll(zw, -1))
        zcour[which] = jnp.broadcast_to(courant, (8, NZ))
        constant_rows(ax_z, 0, courant, zs, lane_roll(zs, -1), steps)

    def merid_constants(slots, steps):
        def row(i, at):
            block, which = (i + 1) // 2, at + (i + 1) % 2
            return winds[0, block, which : which + 1, :]

        for slot in slots:
            face = SLOT_FACE[slot]
            courant = 0.5 * (row(face + 1, 0) + row(face + 2, 0))
            mcour[:, slot * NY : (slot + 1) * NY] = jnp.broadcast_to(courant, (8, NY))
            constant_rows(ax_m, slot * NY, courant, row(face + 1, 2), row(face + 2, 2), steps)

    with mark("prepare"):
        prepare(0)
        conc_out[...] = block_of(conc_ref)
        target_out[...] = block_of(target_ref)
        slab = jnp.concatenate(
            [mwind_ref[0], sea_ref[...].astype(F32), zwind_ref[0], zwind_ref[0]], 0
        )
        wind_out[...] = slab
        line[...] = to_line(*both_rows(conc_out[...]))
        zonal_constants(slab, range(STEPS))
        for acc in (grads, acc3, accb2, accp):
            acc[...] = jnp.zeros_like(acc)
    with mark("zonal"):
        block_out[...] = zonal(0)
    with mark("barrier"):
        pl.semaphore_wait(barrier, greeted)
    move_start(block_out, halo, halo_send, halo_recv, (0, 1, 4))
    move_start(wind_out, winds, wind_send, wind_recv, (0, 1, 4))
    move_start(wind_out, winds, wind_send, wind_recv, (2, 3))
    move_start(block_out, halo, halo_send, halo_recv, (2, 3))
    move_start(target_out, targets, target_send, target_recv, (0, 1, 4))

    @pl.when(moved)
    def _():
        swap_copy(conc_out, conc_in, 0).start()

    @pl.when(jnp.logical_not(moved))
    def _():
        conc_in[...] = conc_out[...]

    with mark("prepare1"):
        prepare(1)
    with mark("waitwind"):
        move_wait(wind_out, winds, wind_send, wind_recv, (0, 1, 4))
    with mark("constants"):
        merid_constants((0, 1, 2, 3, 4), range(STEPS))

        @pl.when(moved)
        def _():
            zonal_constants(winds[0, 2], range(STEPS))

    move_drain(block_out, halo, halo_send, halo_recv, (0, 1, 2, 3, 4))
    zonal_constants(winds[0, 1], (STEPS,), 1)
    zonal_constants(winds[0, 3], (STEPS + 1,), 2)
    with mark("waitmove"):
        move_wait(block_out, halo, halo_send, halo_recv, (0, 1, 4))

    def merid(s):
        with mark("merid"):
            f1, f2, f3 = merid_faces(s, (0, 1, 2))
            new = halo[s, 2] - pick(f2 - f1, f3 - f2)
            line[...] = to_line(*both_rows(new))

    def merid_wide(s, own_flux):
        with mark("merid4"):
            f0, f4, f9, f5 = merid_faces(s, (3, 4, 5, 6))
        f1, f2, f3 = own_flux
        new = halo[s, 2] - pick(f2 - f1, f3 - f2)
        before = halo[s, 1] - pick(f0 - f9, f1 - f0)
        after = halo[s, 3] - pick(f4 - f3, f5 - f4)
        return before, new, after

    def halo_step(s):
        with mark("zonal"):
            halo[s, 2] = zonal(s)
        halo_start(halo, s, halo_send, halo_recv, (0, 1, 2, 3))

    with mark("merid"):
        own_flux = merid_faces(0, (0, 1, 2))
    with mark("waittwo"):
        move_wait(wind_out, winds, wind_send, wind_recv, (2, 3))
        merid_constants((5, 6), (0, STEPS - 1))
        move_wait(block_out, halo, halo_send, halo_recv, (2, 3))
    before, new, after = merid_wide(0, own_flux)
    before = jnp.where(mine > 0, before, 0.0)
    after = jnp.where(mine < bands - 1, after, 0.0)
    with mark("zonal3"):
        blocks = zonal_many(
            [
                (1, 0, to_line(*both_rows(new))),
                (STEPS, 1, to_line(*both_rows(before))),
                (STEPS + 1, 2, to_line(*both_rows(after))),
            ]
        )
    halo[1, 2] = blocks[0]
    halo_start(halo, 1, halo_send, halo_recv, (2, 3))
    halo[1, 1] = blocks[1]
    halo[1, 3] = blocks[2]
    merid(1)
    halo_drain(halo, 1, halo_send, halo_recv, (2, 3))
    halo_step(2)
    with mark("redundant"):
        halo_wait(halo, 1, halo_send, halo_recv, (2, 3))
        merid_faces(1, (3, 4))

    @pl.when(moved)
    def _():
        with mark("zonal_again"):
            swap_copy(conc_out, conc_in, 0).wait_recv()
            line[...] = to_line(*both_rows(conc_in[...]))
            zonal(0)

    move_wait(target_out, targets, target_send, target_recv, (0, 1, 4))
    halo_drain(halo, 2, halo_send, halo_recv, (0, 1, 2, 3))
    with mark("waithalo"):
        halo_wait(halo, 2, halo_send, halo_recv, (0, 1))
    with mark("merid"):
        own_flux = merid_faces(2, (0, 1, 2))
    with mark("waittwo"):
        halo_wait(halo, 2, halo_send, halo_recv, (2, 3))
    before, new, after = merid_wide(2, own_flux)
    ghalo[2, 2] = (new - targets[0, 2]) * loss_scale
    ghalo[2, 1] = jnp.where(mine > 0, (before - targets[0, 1]) * loss_scale, 0.0)
    ghalo[2, 3] = jnp.where(mine < bands - 1, (after - targets[0, 3]) * loss_scale, 0.0)
    final_out[...] = new

    @pl.when(moved)
    def _():
        swap_copy(final_out, final_in, 1).start()

    def merid_back(s):
        @pl.when(s < STEPS - 1)
        def _():
            halo_drain(ghalo, s, ghalo_send, ghalo_recv, (0, 1))
            with mark("waitg"):
                halo_wait(ghalo, s, ghalo_send, ghalo_recv, (0, 1))

        g = []
        for block in (1, 2, 3):
            g.extend(both_rows(ghalo[s, block]))
        lows, highs = [None] * 5, [None] * 5
        first = None
        inner = None
        parts = []
        for slot, face in enumerate(SLOT_FACE[:5]):
            lanes = slice(slot * NY, (slot + 1) * NY)
            part = backward(
                1,
                s,
                lanes,
                g[face + 1] - g[face],
                mcour[:, lanes],
                d1_m,
                d2_m,
                pb_m,
                s1_m,
                s2_m,
                st_m,
                cf_m,
            )
            parts.append(part)
        for slot, (out, weighted) in enumerate(run(parts)):
            face = SLOT_FACE[slot]
            lows[face], highs[face] = out[0:8], out[8:16]
            if slot == 0:
                first = lane_fold(weighted)
            elif slot == 1:
                inner = lane_fold(weighted)
            elif slot == 2:
                inner = inner + lane_fold(weighted)
        new = ghalo[s, 2] + (highs[1] + lows[3])
        new = new + turn(pick(highs[2] + lows[4], highs[0] + lows[2]))
        accp[1] += inner

        @pl.when(mine == 0)
        def _():
            accp[1] += first

        gline[...] = to_line(*both_rows(new))

    def zonal_back(s, last=False, beside=()):
        gz = gline[...]
        dflux = lane_roll(gz, -1) - gz
        outs = run(
            [
                backward(
                    0,
                    s,
                    lanes,
                    dflux[:, lanes],
                    zcour[0, :, lanes],
                    d1_z,
                    d2_z,
                    pb_z,
                    s1_z,
                    s2_z,
                    st_z,
                    cf_z,
                    last,
                )
                for lanes in zchunks
            ]
            + list(beside)
        )[: len(zchunks)]
        accp[0] += sum(lane_fold(o[1]) for o in outs)
        if last:
            return None
        out = jnp.concatenate([o[0] for o in outs], 1)
        low, high = out[0:8], out[8:16]
        t = pick(lane_roll(low, -1), low) + pick(lane_roll(high, 1), lane_roll(high, 2))
        new = gz + t + turn(t)

        return pick(*from_line(new))

    def inner_weights(s):
        return weight_stages(1, s, slice(NY, 3 * NY), ax_m, h2_m, d1_m, d2_m, pb_m)

    def first_face_weights(s):
        @pl.when(mine == 0)
        def _():
            weight_grads(1, s, slice(0, NY), ax_m, h2_m, d1_m, d2_m, pb_m)

    def zonal_weights(s):
        weight_grads(0, s, slice(0, NZ), ax_z, h2_z, d1_z, d2_z, pb_z)

    def backward_step(i, carry):
        s = STEPS - 1 - i
        merid_back(s)
        ghalo[s - 1, 2] = zonal_back(s)
        halo_start(ghalo, s - 1, ghalo_send, ghalo_recv, (0, 1))
        with mark("weights"):
            run([inner_weights(s)])
            zonal_weights(s)
            first_face_weights(s)
        return carry

    lax.fori_loop(0, STEPS - 1, backward_step, 0)

    def groups(x):
        x = x + pltpu.roll(x, 7, axis=0)
        return x + pltpu.roll(x, 6, axis=0)

    def gather_net(net):
        top = net * NET_ROWS
        grads[top + 149 : top + 150] = accb2[net, 20:21, :]
        low, high = groups(acc3[net, 0:8]), groups(acc3[net, 8:16])
        rows = [low[0:1], low[4:5], high[0:1], high[4:5]]
        middle = 0.25 * ((rows[0] + rows[1]) + (rows[2] + rows[3]))
        for j in range(4):
            grads[top + 152 + j : top + 153 + j] = rows[j] - middle

    def gather_bias(net):
        sums = jnp.sum(accp[net], 1, keepdims=True)
        own = (
            lax.broadcasted_iota(jnp.int32, (16, WIDTH), 0) // 4
            == lax.broadcasted_iota(jnp.int32, (16, WIDTH), 1)
        )
        row = jnp.sum(jnp.where(own, sums, 0.0), 0, keepdims=True)
        top = net * NET_ROWS
        grads[top + 156 : top + 157] = row - jnp.sum(row, 1, keepdims=True) * 0.25

    piece = GRAD_ROWS // levs
    part = piece // side_y
    started = []

    def send(src, dst, phase, device):
        pltpu.make_async_remote_copy(
            src_ref=src,
            dst_ref=dst,
            send_sem=red_send.at[phase],
            recv_sem=red_recv.at[phase],
            device_id=device,
            device_id_type=LOGICAL,
        ).start()

    def wait(buf, count, phase):
        with mark("wait_ar"):
            some = buf.at[0:count]
            pltpu.make_async_copy(some, some, red_recv.at[phase]).wait()
        started.append((some, phase))

    wide = levs // 2
    my_x = lax.div(lev, 2)
    core = lev - 2 * my_x

    def first_copy(net, k):
        tx = wrap(my_x + k, wide)
        slot = 2 * k + core
        row = pl.multiple_of(net * NET_ROWS + tx * piece, 8)
        return pltpu.make_async_remote_copy(
            src_ref=grads.at[pl.ds(row, piece)],
            dst_ref=r1.at[slot],
            send_sem=red_send.at[0],
            recv_sem=red_recv.at[0],
            device_id=lev_device(2 * tx + net),
            device_id_type=LOGICAL,
        )

    def send_net(net):
        for k in far_first(wide):
            first_copy(net, k).start()

        @pl.when(core != net)
        def _():
            first_copy(net, 0).start()

    merid_back(0)
    with mark("zback0"):
        zonal_back(0, True, [inner_weights(0)])
    with mark("wg1"):
        first_face_weights(0)
    with mark("gather1"):
        gather_bias(1)
        gather_bias(0)
        gather_net(1)
        send_net(1)
    with mark("wg0"):
        zonal_weights(0)
    with mark("gather0"):
        gather_net(0)
        send_net(0)
    @pl.when(moved)
    def _():
        swap_copy(final_out, final_in, 1).wait()
        swap_copy(conc_out, conc_in, 0).wait_send()

    final = jnp.where(moved, final_in[...], final_out[...])
    for r in range(2):
        for b in range(4):
            field_ref[b, 0, r : r + 1, :] = final[4 * r + b : 4 * r + b + 1, :]
    move_drain(wind_out, winds, wind_send, wind_recv, (0, 1, 2, 3, 4))
    move_drain(target_out, targets, target_send, target_recv, (0, 1, 4))

    row = pl.multiple_of(core * NET_ROWS + my_x * piece, 8)
    with mark("wait_ar"):
        wait(r1, levs - 1, 0)
        total = grads[pl.ds(row, piece)] + r1[1 - core]
        for k in range(1, wide):
            for c in range(2):
                total = total + r1[2 * k + c]
    for i in range(side_y):
        s1buf[i] = total[i * part : (i + 1) * part]
    for d in far_first(side_y):
        ty = wrap(my_y + d, side_y)
        send(s1buf.at[ty], r2.at[d - 1], 1, y_device(ty))
    total = s1buf[my_y]
    wait(r2, side_y - 1, 1)
    for d in range(1, side_y):
        total = total + r2[d - 1]
    r3[my_z] = total
    for d in far_first(side_z):
        tz = wrap(my_z + d, side_z)
        send(r3.at[my_z], r3.at[my_z], 2, z_device(tz))
    wait(r3, side_z - 1, 2)
    total = r3[0]
    for i in range(1, side_z):
        total = total + r3[i]
    a4[my_y] = total
    for d in far_first(side_y):
        ty = wrap(my_y + d, side_y)
        send(a4.at[my_y], a4.at[my_y], 3, y_device(ty))
    wait(a4, side_y - 1, 3)
    for i in range(side_y):
        full[lev, i * part : (i + 1) * part] = a4[i]
    for d in sorted(range(1, levs), key=lambda d: -min(d // 2, wide - d // 2)):
        tl = wrap(lev + d, levs)
        send(full.at[lev], full.at[lev], 4, lev_device(tl))
    wait(full, levs - 1, 4)
    for net in range(2):
        everything = jnp.concatenate([full[2 * x + net] for x in range(wide)], 0)
        top = 0
        gw2_ref[net] = everything[top : top + 128]
        gw1_ref[:, net, :] = everything[top + 128 : top + 148]
        gb1_ref[net : net + 1] = everything[top + 148 : top + 149]
        gb2_ref[net : net + 1] = everything[top + 149 : top + 150]
        gw3_ref[net] = everything[top + 152 : top + 156]
        gb3_ref[net : net + 1] = everything[top + 156 : top + 157, 0:4]

    for some, phase in started:
        pltpu.make_async_copy(some, some, red_send.at[phase]).wait()


def on_device(bands, levs, loss_scale, *args):
    piece = GRAD_ROWS // levs
    side_y = math.isqrt(bands)
    side_z = bands // side_y
    part = piece // side_y
    vmem = pltpu.VMEM
    saved = [(STEPS + 2, NZ), (STEPS, NM)]
    back = [NZ, NB]
    args = list(args)
    args[5] = jnp.transpose(args[5], (1, 0, 2))
    scratch = [
        *[vmem(arg.shape, arg.dtype) for arg in args],
        pltpu.SemaphoreType.DMA((len(args),)),
        vmem((2, 128, 128), BF16),
        vmem((2, 256, 256), BF16),
        vmem((2, 32, 256), BF16),
        vmem((2, 128, 128), BF16),
        vmem((2, 256, 256), BF16),
        vmem((2, 32, 256), BF16),
        vmem((2, 128, 128), F32),
        vmem((2, 16, 128), F32),
        vmem((3, 8, NZ), F32),
        vmem((8, NM), F32),
        vmem((STEPS, 5, 8, NY), F32),
        vmem((STEPS, 5, 8, NY), F32),
        vmem((1, 5, 8, NY), F32),
        vmem((8, NY), F32),
        vmem((8, NY), F32),
        vmem((8, NY), F32),
        vmem((8, NY), F32),
        vmem((8, NY), F32),
        vmem((1, 5, 8, NY), F32),
        vmem((8, NY), F32),
        vmem((8, NY), F32),
        vmem((8, NZ), F32),
        vmem((8, NZ), F32),
        *[vmem((k, 352, n), BF16) for k, n in saved],
        *[vmem((k, 256, n), BF16) for k, n in saved],
        *[vmem((k, 128, n), F32) for k, n in saved],
        *[vmem((k, 128, n), F32) for k, n in saved],
        *[vmem((k, 16, n), F32) for k, n in saved],
        *[vmem((k, 16, n), F32) for k, n in saved],
        *[vmem((256, n), BF16) for n in back],
        *[vmem((256, n), BF16) for n in back],
        *[vmem((32, n), BF16) for n in back],
        vmem((2, 16, 128), F32),
        vmem((2, 32, 128), F32),
        vmem((2, 16, 128), F32),
        vmem((GRAD_ROWS, 128), F32),
        vmem((levs, piece, 128), F32),
        vmem((side_y, part, 128), F32),
        vmem((side_y - 1, part, 128), F32),
        vmem((side_z, part, 128), F32),
        vmem((side_y, part, 128), F32),
        vmem((levs, piece, 128), F32),
        pltpu.SemaphoreType.DMA((5,)),
        pltpu.SemaphoreType.DMA((STEPS, 5)),
        pltpu.SemaphoreType.DMA((2,)),
        pltpu.SemaphoreType.DMA((STEPS, 2)),
        pltpu.SemaphoreType.DMA((5,)),
        pltpu.SemaphoreType.DMA((1, 5)),
        pltpu.SemaphoreType.DMA((5,)),
        pltpu.SemaphoreType.DMA((1, 5)),
        pltpu.SemaphoreType.DMA((2,)),
        pltpu.SemaphoreType.DMA((2,)),
        pltpu.SemaphoreType.DMA((5,)),
        pltpu.SemaphoreType.DMA((5,)),
    ]
    out_shape = [jax.ShapeDtypeStruct(args[0].shape, F32)] + [
        jax.ShapeDtypeStruct(args[i].shape, F32) for i in range(5, 11)
    ]
    results = pl.pallas_call(
        functools.partial(kernel, bands, levs, loss_scale),
        out_shape=out_shape,
        in_specs=[pl.BlockSpec(memory_space=pltpu.HBM)] * 11,
        out_specs=[pl.BlockSpec(memory_space=pltpu.VMEM)] * 7,
        scratch_shapes=scratch,
        compiler_params=pltpu.CompilerParams(
            collective_id=0, has_side_effects=True, vmem_limit_bytes=48 * 1024 * 1024
        ),
        name="advection_step",
    )(*[pltpu.with_memory_space_constraint(arg, pltpu.HBM) for arg in args])
    results = list(
        pl.pallas_call(
            write_out,
            out_shape=out_shape,
            in_specs=[pl.BlockSpec(memory_space=pltpu.VMEM)] * 7,
            out_specs=[pl.BlockSpec(memory_space=pltpu.HBM)] * 7,
            scratch_shapes=[pltpu.SemaphoreType.DMA((7,))],
            compiler_params=pltpu.CompilerParams(vmem_limit_bytes=1024 * 1024),
            name="write_out",
        )(*results)
    )
    results[1] = jnp.transpose(results[1], (1, 0, 2))
    return tuple(results)


def write_out(*refs):
    sem = refs[14]
    copies = [pltpu.make_async_copy(refs[i], refs[7 + i], sem.at[i]) for i in range(7)]
    for copy in copies:
        copy.start()
    for copy in copies:
        copy.wait()


def solution(mesh):
    bands, levs = mesh.shape["band"], mesh.shape["lev"]
    loss_scale = 1.0 / math.sqrt(4 * levs * 2 * bands * NY)
    return jax.shard_map(
        functools.partial(on_device, bands, levs, loss_scale),
        mesh=mesh,
        in_specs=(
            P(None, "lev", "band", None),
            P(None, "lev", "band", None),
            P("lev", "band", None),
            P("lev", "band", None),
            P("band", None),
            P(),
            P(),
            P(),
            P(),
            P(),
            P(),
        ),
        out_specs=(P(None, "lev", "band", None), P(), P(), P(), P(), P(), P()),
        check_vma=False,
    )
```
